32 devices in a mesh: row: 4 (over y, core), col: 4 (over z), dp: 2 (over x).
Axes of the slice: x: 2, y: 2, z: 4, core: 2. Of those that a mesh axis runs over, the one named last changes fastest.
Arguments:
- features: bfloat16 [1024, 512, 128], P(('dp', 'row'), 'col'), parts along dimension 0, may hold values from -6 to 6
- labels: int32 [1024, 512], P(('dp', 'row', 'col')), parts along dimension 0, may hold values from 0 to 63
- norm_gain: float32 [3, 128], replicated, may hold values from 0.5 to 1.5
- w_down: bfloat16 [2, 128, 64], replicated, may hold values from -0.5 to 0.5
- w_conv: bfloat16 [2, 3, 3, 64, 64], replicated, may hold values from -0.25 to 0.25
- w_up: bfloat16 [2, 64, 128], replicated, may hold values from -0.75 to 0.75
- w_head: bfloat16 [128, 64], replicated, may hold values from -0.5 to 0.5
- head_bias: float32 [64], replicated, may hold values from -4 to 4
Outputs:
- grad_input: float32 [1024, 512, 128], P(('dp', 'row'), 'col'), parts along dimension 0
The draws below stay inside these ranges and needn't reach their ends.
There are 2 independent parts, one for each index of `dp`. The reference program is written for one: setup_inputs(seed, part) draws one part's arguments, and reference() takes and returns one part's arrays. A program takes and returns all parts, laid end to end along the dimension named above; an argument that names none is the same for every part. Nothing has to cross between parts.
All inputs are finite; a program needn't handle non-finite values.
Results may differ from the reference program's by a relative error of at most 0.0095.
Values may be sent and summed in bfloat16 or wider, within the bound.
No kernel may reach another device: no remote copies, remote signals or barrier semaphores. Data moves between devices by JAX's collectives and lax.ppermute only.
A program may use at most 192 MiB of HBM per device.

```python
import jax
import jax.numpy as jnp
from jax import lax

L = 512
C = 128
CB = 64
NB = 64


def place_ends(result, own_key, low, top_value):
    place = [jax.random.randint(jax.random.fold_in(own_key, axis), (), 0, length) for axis, length in enumerate(result.shape)]
    widest = result.shape.index(max(result.shape))
    neighbour = place[:widest] + [(place[widest] + 1) % result.shape[widest]] + place[widest + 1:]
    return result.at[tuple(place)].set(low).at[tuple(neighbour)].set(top_value)


def shard_levels(key, shape, pieces, least, largest):
    factor_of = 1.0
    for dim, parts in pieces:
        draws = jax.random.uniform(jax.random.fold_in(jax.random.fold_in(key, 6), dim), (parts,), jnp.float32, least / len(pieces), largest / len(pieces))
        factor_of = factor_of * jnp.repeat(jnp.exp(draws), shape[dim] // parts).reshape((-1,) + (1,) * (len(shape) - 1 - dim))
    return factor_of


def gaussian(key, extent, scale, limit, split=(), kind=jnp.bfloat16):
    result = scale * jax.random.normal(key, extent, jnp.float32)
    if split:
        result = result * shard_levels(key, extent, split, -0.22, 0.18)
    return jnp.clip(result, -limit, limit).astype(kind)


def setup_inputs(seed: int = 0, part: int = 0) -> dict:
    arg_keys = jax.random.split(jax.random.key(seed), 9)
    part_keys = jax.random.split(jax.random.fold_in(arg_keys[8], part), 9)
    features = gaussian(part_keys[0], (L, L, C), 1.0, 6.0, ((0, 4), (1, 4)))
    labels = place_ends(jax.random.randint(part_keys[1], (L, L), 0, NB), jax.random.fold_in(part_keys[1], 1), 0, NB - 1).astype(jnp.int32)
    norm_gain = jnp.clip(jax.random.uniform(arg_keys[2], (3, C), jnp.float32, 0.5, 1.5), 0.5, 1.5)
    w_down = gaussian(arg_keys[3], (2, C, CB), C ** -0.5, 0.5)
    w_conv = gaussian(arg_keys[4], (2, 3, 3, CB, CB), (9 * CB) ** -0.5, 0.25)
    w_up = gaussian(arg_keys[5], (2, CB, C), CB ** -0.5, 0.75)
    w_head = gaussian(arg_keys[6], (C, NB), C ** -0.5, 0.5)
    head_bias = gaussian(arg_keys[7], (NB,), 1.0, 4.0, (), jnp.float32)
    return dict(features=features, labels=labels, norm_gain=norm_gain, w_down=w_down, w_conv=w_conv, w_up=w_up, w_head=w_head, head_bias=head_bias)


epsilon = 1e-05

def normalize(values, scales):
    average = lax.optimization_barrier(jnp.mean(values, -1, keepdims=True))
    centred = values - average
    variance = lax.optimization_barrier(jnp.mean(centred * centred, -1, keepdims=True))
    return centred * lax.rsqrt(variance + epsilon) * scales

def normalize_back(values, scales, upstream):
    unused, pullback = jax.vjp(lambda argument: normalize(argument, scales), values)
    return pullback(upstream)[0]

def elu_forward(values):
    return jnp.where(values > 0, values, jnp.expm1(jnp.minimum(values, 0.0)))

def elu_slope(values):
    return jnp.where(values > 0, 1.0, jnp.exp(jnp.minimum(values, 0.0)))

def bottleneck_in(stream, scales, down_weight):
    normed = normalize(stream, scales)
    lowered = jnp.dot(elu_forward(normed).astype(jnp.bfloat16), down_weight, preferred_element_type=jnp.float32)
    return (elu_forward(lowered).astype(jnp.bfloat16), normed, lowered)

def dilated(padded, kernel, spacing, row_count, col_count, mirrored):
    summed = jnp.zeros((row_count, col_count, kernel.shape[-1]), jnp.float32)
    for row_tap in range(3):
        for col_tap in range(3):
            if mirrored:
                start_row = (2 - row_tap) * spacing
                start_col = (2 - col_tap) * spacing
                weight = kernel[row_tap, col_tap].T
            else:
                start_row = row_tap * spacing
                start_col = col_tap * spacing
                weight = kernel[row_tap, col_tap]
            window = padded[start_row:start_row + row_count, start_col:start_col + col_count]
            summed = summed + jnp.dot(window, weight, preferred_element_type=jnp.float32)
    return summed

def bottleneck_out(convolved, up_weight):
    return jnp.dot(elu_forward(convolved).astype(jnp.bfloat16), up_weight, preferred_element_type=jnp.float32)

def block_back(upstream, saved_state, scales, down_weight, kernel, up_weight, spacing, widen):
    stream, normed, lowered, convolved = saved_state
    activated = jnp.dot(upstream.astype(jnp.bfloat16), up_weight.T, preferred_element_type=jnp.float32)
    conv_grad = (activated * elu_slope(convolved)).astype(jnp.bfloat16)
    padded = widen(conv_grad, spacing)
    lowered_grad = dilated(padded, kernel, spacing, conv_grad.shape[0], conv_grad.shape[1], True) * elu_slope(lowered)
    normed_grad = jnp.dot(lowered_grad.astype(jnp.bfloat16), down_weight.T, preferred_element_type=jnp.float32) * elu_slope(normed)
    return upstream + normalize_back(stream, scales, normed_grad)

def widen_map(values, spacing):
    return jnp.pad(values, ((spacing, spacing), (spacing, spacing), (0, 0)))

def reference(features, labels, norm_gain, w_down, w_conv, w_up, w_head, head_bias):
    stream = features.astype(jnp.float32)
    stored = []
    for section_index, spacing in ((0, 4), (1, 8)):
        squeezed, normed, lowered = bottleneck_in(stream, norm_gain[section_index], w_down[section_index])
        convolved = dilated(widen_map(squeezed, spacing), w_conv[section_index], spacing, L, L, False)
        stored.append((stream, normed, lowered, convolved))
        stream = stream + bottleneck_out(convolved, w_up[section_index])
    head_in = normalize(stream, norm_gain[2]).astype(jnp.bfloat16)
    logits = (jnp.dot(head_in, w_head, preferred_element_type=jnp.float32) + head_bias).astype(jnp.bfloat16)
    symmetric = 0.5 * (logits.astype(jnp.float32) + jnp.swapaxes(logits, 0, 1).astype(jnp.float32))
    exponent = jnp.exp(symmetric)
    probability = exponent / lax.optimization_barrier(jnp.sum(exponent, -1, keepdims=True))
    onehot = (labels[:, :, None] == jnp.arange(NB, dtype=jnp.int32)).astype(jnp.float32)
    sym_grad = probability - onehot
    logit_grad = (0.5 * (sym_grad + jnp.swapaxes(sym_grad, 0, 1))).astype(jnp.bfloat16)
    head_grad = jnp.dot(logit_grad, w_head.T, preferred_element_type=jnp.float32)
    stream_grad = normalize_back(stream, norm_gain[2], head_grad)
    for section_index, spacing in ((1, 8), (0, 4)):
        stream_grad = block_back(stream_grad, stored[section_index], norm_gain[section_index], w_down[section_index], w_conv[section_index], w_up[section_index], spacing, widen_map)
    return stream_grad
```

```python
import functools

import jax
import jax.numpy as jnp
from jax import lax
from jax.experimental import pallas as pl
from jax.experimental.pallas import tpu as pltpu
from jax.sharding import PartitionSpec as P

epsilon = 1e-05
F32 = jnp.float32
BF16 = jnp.bfloat16
ROWS = 4
EDGE = 8
PAD = 16


def lane_low(shape):
    return lax.broadcasted_iota(jnp.int32, shape, len(shape) - 1) < shape[-1] // 2


def standardize(values):
    centred = values - jnp.mean(values, -1, keepdims=True)
    variance = jnp.mean(centred * centred, -1, keepdims=True)
    inverse = lax.rsqrt(variance + epsilon)
    return centred * inverse, inverse


def elu(values):
    return jnp.where(values > 0, values, jnp.exp(jnp.minimum(values, 0.0)) - 1.0)


def slope_of(values):
    return jnp.where(values > 0, 1.0, jnp.exp(jnp.minimum(values, 0.0)))


def slope_from_elu(activated):
    return 1.0 + jnp.minimum(activated, 0.0)


def standardize_back(standard, inverse, upstream):
    along = jnp.mean(upstream, -1, keepdims=True)
    across = jnp.mean(upstream * standard, -1, keepdims=True)
    return inverse * (upstream - along - standard * across)


def squeeze(stream, gain, down):
    standard, unused = standardize(stream)
    entered = elu(standard * gain).astype(BF16)
    return elu(jnp.dot(entered, down, preferred_element_type=F32))


def store_edges(values, refs, spacing, step, steps):
    top, bottom, left, right, corner_a, corner_b, corner_c, corner_d = refs
    columns = values.shape[2]
    low = lane_low((ROWS, EDGE, values.shape[3]))
    left[...] = jnp.where(low, values[0, :, :EDGE], values[1, :, :EDGE]).astype(BF16)
    right[...] = jnp.where(low, values[0, :, columns - EDGE :], values[1, :, columns - EDGE :]).astype(BF16)
    wide = lane_low((ROWS, columns // 2, values.shape[3]))
    taken = spacing // ROWS

    @pl.when(step < taken)
    def _():
        top[...] = jnp.where(wide, values[0, :, : columns // 2], values[0, :, columns // 2 :]).astype(BF16)
        corner_a[...] = values[0, :, :EDGE].astype(BF16)
        corner_b[...] = values[0, :, columns - EDGE :].astype(BF16)

    @pl.when(step >= steps - taken)
    def _():
        bottom[...] = jnp.where(wide, values[1, :, : columns // 2], values[1, :, columns // 2 :]).astype(BF16)
        corner_c[...] = values[1, :, :EDGE].astype(BF16)
        corner_d[...] = values[1, :, columns - EDGE :].astype(BF16)


def fill_padded(padded, centre, halos, spacing):
    above, below, before, after, corner_a, corner_b, corner_c, corner_d = halos
    rows, columns, lanes = centre.shape
    half = rows // 2

    def lay(row, carry):
        padded[spacing + row, PAD : PAD + columns] = centre[row]
        return carry

    lax.fori_loop(0, rows, lay, 0)

    def twice(packed):
        turned = pltpu.roll(packed, lanes // 2, packed.ndim - 1)
        low = lane_low(packed.shape)
        return jnp.where(low, packed, turned).astype(BF16), jnp.where(low, turned, packed).astype(BF16)

    def sides(row, carry):
        for halo, start in ((before, PAD - EDGE), (after, PAD + columns)):
            first, second = twice(halo[row].astype(F32))
            padded[spacing + row, start : start + EDGE] = first
            padded[spacing + half + row, start : start + EDGE] = second
        return carry

    lax.fori_loop(0, half, sides, 0)
    for halo, one, two, base in ((above, corner_a, corner_b, 0), (below, corner_c, corner_d, spacing + rows)):
        for row in range(spacing):
            first, second = twice(halo[row].astype(F32))
            padded[base + row, PAD : PAD + columns // 2] = first
            padded[base + row, PAD + columns // 2 : PAD + columns] = second
            padded[base + row, PAD - EDGE : PAD] = one[row]
            padded[base + row, PAD + columns : PAD + columns + EDGE] = two[row]


def convolve(padded, kernel, taps, spacing, step, half, columns):
    width = columns + 2 * PAD
    lanes = padded.shape[2]
    low = lane_low((ROWS, width, lanes))
    parts = []
    for side in range(2):
        start = side * half + step * ROWS
        first, second, third = (padded[pl.ds(start + tap * spacing, ROWS)] for tap in range(3))
        parts.append(jnp.concatenate([jnp.where(low, first, second), third], axis=2))
    joined = jnp.concatenate(parts, axis=0).reshape(2 * ROWS * width, 2 * lanes)
    taps[...] = jnp.dot(joined, kernel[...], preferred_element_type=F32).reshape(2 * ROWS, width, 3 * lanes)
    total = taps[:, PAD : PAD + columns, lanes : 2 * lanes]
    total = total + taps[:, PAD - spacing : PAD - spacing + columns, :lanes]
    total = total + taps[:, PAD + spacing : PAD + spacing + columns, 2 * lanes :]
    return total.reshape(2 * ROWS * columns, lanes)


def strip(reference):
    return reference[...].reshape(-1, reference.shape[-1])


def entry_kernel(spacing, steps, features, gain, down, squeezed, *edges):
    step = pl.program_id(0)
    values = squeeze(strip(features).astype(F32), gain[...], down[...]).reshape(squeezed.shape)
    squeezed[...] = values.astype(BF16)
    store_edges(values, edges, spacing, step, steps)


def middle_kernel(near, far, steps, centre, *rest):
    halos, rest = rest[:8], rest[8:]
    features, kernel, up, gain, down, stream_out, activated_out, squeezed, *rest = rest
    edges, (padded, taps) = rest[:8], rest[8:]
    step = pl.program_id(0)
    half, columns = centre.shape[0] // 2, centre.shape[1]

    @pl.when(step == 0)
    def _():
        fill_padded(padded, centre, halos, near)

    activated = elu(convolve(padded, kernel, taps, near, step, half, columns)).astype(BF16)
    activated_out[...] = activated.reshape(activated_out.shape)
    stream = strip(features).astype(F32) + jnp.dot(activated, up[...], preferred_element_type=F32)
    stream_out[...] = stream.reshape(stream_out.shape)
    values = squeeze(stream, gain[...], down[...]).reshape(squeezed.shape)
    squeezed[...] = values.astype(BF16)
    store_edges(values, edges, far, step, steps)


def head_kernel(near, steps, centre, *rest):
    halos, rest = rest[:8], rest[8:]
    stream_in, kernel, up, gain, head, bias, stream_out, activated_out, by_row, by_column, padded, taps = rest
    step = pl.program_id(0)
    half, columns = centre.shape[0] // 2, centre.shape[1]

    @pl.when(step == 0)
    def _():
        fill_padded(padded, centre, halos, near)

    activated = elu(convolve(padded, kernel, taps, near, step, half, columns)).astype(BF16)
    activated_out[...] = activated.reshape(activated_out.shape)
    stream = strip(stream_in) + jnp.dot(activated, up[...], preferred_element_type=F32)
    stream_out[...] = stream.reshape(stream_out.shape)
    standard, unused = standardize(stream)
    entered = (standard * gain[...]).astype(BF16).reshape(2, ROWS, columns, stream.shape[1])
    pairs = jnp.concatenate([entered[0], entered[1]], axis=2).reshape(ROWS * columns, -1)
    logits = jnp.dot(pairs, head[...], preferred_element_type=F32) + bias[...]
    by_row[...] = logits.astype(BF16).reshape(by_row.shape)
    pairs = jnp.concatenate([entered[:, :, : columns // 2], entered[:, :, columns // 2 :]], axis=3)
    logits = jnp.dot(pairs.reshape(ROWS * columns, -1), head[...], preferred_element_type=F32) + bias[...]
    by_column[...] = logits.astype(BF16).reshape(by_column.shape)


def loss_kernel(
    spacing, steps, by_row, facing, targets, stream, activated, gain, head, group, up, grad_out, conv_out, *rest
):
    edges, (turned,) = rest[:8], rest[8:]
    step = pl.program_id(0)
    inner = facing.shape[1] // ROWS

    @pl.when(step % inner == 0)
    def _():
        turned[...] = jnp.swapaxes(facing[...].astype(F32), 0, 1)

    start = (step % inner) * ROWS
    columns, lanes = by_row.shape[1:]
    symmetric = 0.5 * (by_row[...].astype(F32) + turned[pl.ds(start, ROWS)])
    exponent = jnp.exp(symmetric).reshape(ROWS * columns, lanes)
    upper = exponent.astype(BF16)
    lower = (exponent - upper.astype(F32)).astype(BF16)
    total = jnp.dot(upper, group[...], preferred_element_type=F32) + jnp.dot(
        lower, group[...], preferred_element_type=F32
    )
    logit_grad = (exponent / total - targets[...].astype(F32).reshape(exponent.shape)).astype(BF16)
    back = jnp.dot(logit_grad, head[...], preferred_element_type=F32)
    width = back.shape[1] // 2
    back = jnp.concatenate([back[:, :width], back[:, width:]], axis=0)
    standard, inverse = standardize(strip(stream))
    grad = standardize_back(standard, inverse, back * gain[...])
    grad_out[...] = grad.reshape(grad_out.shape)
    values = jnp.dot(grad.astype(BF16), up[...], preferred_element_type=F32)
    values = values * slope_from_elu(strip(activated).astype(F32))
    values = values.reshape(conv_out.shape)
    conv_out[...] = values.astype(BF16)
    store_edges(values, edges, spacing, step, steps)


def back_strip(spacing, step, centre, padded, taps, kernel, squeezed, down, stream, gain, upstream):
    half, columns = centre.shape[0] // 2, centre.shape[1]
    lowered = convolve(padded, kernel, taps, spacing, step, half, columns)
    lowered = lowered * slope_from_elu(strip(squeezed).astype(F32))
    entered = jnp.dot(lowered.astype(BF16), down[...], preferred_element_type=F32)
    standard, inverse = standardize(strip(stream).astype(F32))
    entered = entered * slope_of(standard * gain[...])
    return strip(upstream) + standardize_back(standard, inverse, entered * gain[...])


def back_kernel(near, far, steps, centre, *rest):
    halos, rest = rest[:8], rest[8:]
    kernel, squeezed, down, stream, gain, upstream, activated, up, grad_out, conv_out, *rest = rest
    edges, (padded, taps) = rest[:8], rest[8:]
    step = pl.program_id(0)

    @pl.when(step == 0)
    def _():
        fill_padded(padded, centre, halos, near)

    grad = back_strip(near, step, centre, padded, taps, kernel, squeezed, down, stream, gain, upstream)
    grad_out[...] = grad.reshape(grad_out.shape)
    values = jnp.dot(grad.astype(BF16), up[...], preferred_element_type=F32)
    values = values * slope_from_elu(strip(activated).astype(F32))
    values = values.reshape(conv_out.shape)
    conv_out[...] = values.astype(BF16)
    store_edges(values, edges, far, step, steps)


def final_kernel(near, centre, *rest):
    halos, rest = rest[:8], rest[8:]
    kernel, squeezed, down, stream, gain, upstream, grad_out, padded, taps = rest
    step = pl.program_id(0)

    @pl.when(step == 0)
    def _():
        fill_padded(padded, centre, halos, near)

    grad = back_strip(near, step, centre, padded, taps, kernel, squeezed, down, stream, gain, upstream)
    grad_out[...] = grad.reshape(grad_out.shape)


def shifted(values, row_move, col_move):
    rows, cols = lax.axis_size("row"), lax.axis_size("col")
    pairs = []
    for row in range(rows):
        for col in range(cols):
            if 0 <= row + row_move < rows and 0 <= col + col_move < cols:
                pairs.append((row * cols + col, (row + row_move) * cols + col + col_move))
    return lax.ppermute(values, ("row", "col"), pairs)


def exchange(edges):
    top, bottom, left, right, corner_a, corner_b, corner_c, corner_d = edges
    return (
        shifted(bottom, 1, 0),
        shifted(top, -1, 0),
        shifted(right, 0, 1),
        shifted(left, 0, -1),
        shifted(corner_d, 1, 1),
        shifted(corner_c, 1, -1),
        shifted(corner_b, -1, 1),
        shifted(corner_a, -1, -1),
    )


def facing_tile(tile):
    rows, cols = lax.axis_size("row"), lax.axis_size("col")
    if rows == cols:
        pairs = [(row * cols + col, col * cols + row) for row in range(rows) for col in range(cols)]
        return lax.ppermute(tile, ("row", "col"), pairs)
    if cols % rows:
        raise ValueError("unsupported mesh")
    times = cols // rows
    height = tile.shape[0] // times
    place = lax.axis_index("col") % times
    received = []
    for turn in range(times):
        piece = lax.dynamic_slice_in_dim(tile, ((place + turn) % times) * height, height, axis=0)
        pairs = [
            (row * cols + col, (col // times) * cols + times * row + (col % times + turn) % times)
            for row in range(rows)
            for col in range(cols)
        ]
        received.append(lax.ppermute(piece, ("row", "col"), pairs))
    stacked = jnp.stack(received)
    pieces = [
        lax.dynamic_index_in_dim(stacked, (place - source) % times, axis=0, keepdims=False)
        for source in range(times)
    ]
    return jnp.concatenate(pieces, axis=1)


def facing_logits(by_column):
    if lax.axis_size("row") == lax.axis_size("col"):
        return facing_tile(by_column)
    bins = by_column.shape[2] // 2
    tile = facing_tile(jnp.concatenate([by_column[..., :bins], by_column[..., bins:]], axis=1))
    half = tile.shape[1] // 2
    return jnp.concatenate([tile[:, :half], tile[:, half:]], axis=2)


def dilated_weights(kernel):
    twice = jnp.concatenate([kernel, kernel], axis=3)
    flat = jnp.transpose(twice, (0, 2, 1, 3)).reshape(3 * kernel.shape[2], -1)
    return jnp.pad(flat, ((0, kernel.shape[2]), (0, 0)))


def mirrored(kernel):
    return jnp.swapaxes(kernel[::-1, ::-1], 2, 3)


def doubled_columns(weight):
    return jnp.concatenate([weight, weight], axis=1)


def padded_rows(weight):
    return jnp.pad(weight, ((0, weight.shape[0]), (0, 0)))


def diagonal(weight):
    zeros = jnp.zeros_like(weight)
    return jnp.concatenate(
        [jnp.concatenate([weight, zeros], axis=1), jnp.concatenate([zeros, weight], axis=1)], axis=0
    )


def shards(features, labels, norm_gain, w_down, w_conv, w_up, w_head, head_bias):
    rows, columns, channels = features.shape
    narrow = w_down.shape[2]
    bins = w_head.shape[1]
    half = rows // 2
    steps = half // ROWS
    lanes = 2 * narrow
    near, far = 4, 8

    gains = [norm_gain[index : index + 1] for index in range(3)]
    downs = [doubled_columns(w_down[index]) for index in range(2)]
    downs_back = [padded_rows(w_down[index].T) for index in range(2)]
    ups = [padded_rows(w_up[index]) for index in range(2)]
    ups_back = [doubled_columns(w_up[index].T) for index in range(2)]
    convs = [dilated_weights(w_conv[index]) for index in range(2)]
    convs_back = [dilated_weights(mirrored(w_conv[index])) for index in range(2)]
    head = diagonal(w_head)
    head_back = diagonal(w_head.T)
    bias = jnp.concatenate([head_bias, head_bias])[None]
    group = diagonal(jnp.ones((bins, bins), BF16))

    def whole(array):
        zeros = (0,) * array.ndim
        return pl.BlockSpec(array.shape, lambda step: zeros)

    def strip_spec(width):
        return pl.BlockSpec((2, ROWS, columns, width), lambda step: (0, step, 0, 0))

    def halves(dtype, width):
        return jax.ShapeDtypeStruct((2, half, columns, width), dtype)

    def edges(spacing):
        taken = spacing // ROWS
        first = lambda step: (jnp.minimum(step, taken - 1), 0, 0)
        last = lambda step: (jnp.maximum(step - (steps - taken), 0), 0, 0)
        each = lambda step: (step, 0, 0)
        entries = [
            ((spacing, columns // 2, lanes), first),
            ((spacing, columns // 2, lanes), last),
            ((half, EDGE, lanes), each),
            ((half, EDGE, lanes), each),
            ((spacing, EDGE, lanes), first),
            ((spacing, EDGE, lanes), first),
            ((spacing, EDGE, lanes), last),
            ((spacing, EDGE, lanes), last),
        ]
        shapes = [jax.ShapeDtypeStruct(shape, BF16) for shape, index in entries]
        specs = [pl.BlockSpec((ROWS,) + shape[1:], index) for shape, index in entries]
        return shapes, specs

    def scratch(spacing):
        width = columns + 2 * PAD
        return [
            pltpu.VMEM((rows + 2 * spacing, width, lanes), BF16),
            pltpu.VMEM((2 * ROWS, width, 3 * lanes), F32),
        ]

    def cost(convolutions, passes):
        pixels = rows * columns
        return pl.CostEstimate(
            flops=pixels * (convolutions * 18 * narrow * narrow + 4 * narrow * channels),
            bytes_accessed=pixels * channels * passes,
            transcendentals=pixels * channels,
        )

    def call(body, inputs, specs, shapes, out_specs, scratch_shapes, estimate, name):
        return pl.pallas_call(
            body,
            grid=(steps,),
            in_specs=specs,
            out_specs=out_specs,
            out_shape=shapes,
            scratch_shapes=scratch_shapes,
            compiler_params=pltpu.CompilerParams(vmem_limit_bytes=56 * 1024 * 1024),
            cost_estimate=estimate,
            name=name,
        )(*inputs)

    split = features.reshape(2, half, columns, channels)
    bf_spec = strip_spec(channels)
    near_shapes, near_specs = edges(near)
    far_shapes, far_specs = edges(far)

    squeezed_1, *sent = call(
        functools.partial(entry_kernel, near, steps),
        (split, gains[0], downs[0]),
        [bf_spec, whole(gains[0]), whole(downs[0])],
        [halves(BF16, lanes)] + near_shapes,
        [strip_spec(lanes)] + near_specs,
        [],
        cost(0, 4),
        "entry",
    )
    halos = exchange(sent)

    def tile(array):
        return array.reshape(rows, columns, array.shape[-1])

    centre = tile(squeezed_1)
    stream_1, activated_1, squeezed_2, *sent = call(
        functools.partial(middle_kernel, near, far, steps),
        (centre, *halos, split, convs[0], ups[0], gains[1], downs[1]),
        [whole(centre)] + [whole(halo) for halo in halos] + [bf_spec]
        + [whole(array) for array in (convs[0], ups[0], gains[1], downs[1])],
        [halves(F32, channels), halves(BF16, lanes), halves(BF16, lanes)] + far_shapes,
        [strip_spec(channels), strip_spec(lanes), strip_spec(lanes)] + far_specs,
        scratch(near),
        cost(1, 12),
        "middle",
    )
    halos = exchange(sent)

    centre = tile(squeezed_2)
    by_row_spec = pl.BlockSpec((ROWS, columns, 2 * bins), lambda step: (step, 0, 0))
    stream_2, activated_2, by_row, by_column = call(
        functools.partial(head_kernel, far, steps),
        (centre, *halos, stream_1, convs[1], ups[1], gains[2], head, bias),
        [whole(centre)] + [whole(halo) for halo in halos] + [bf_spec]
        + [whole(array) for array in (convs[1], ups[1], gains[2], head, bias)],
        [
            halves(F32, channels),
            halves(BF16, lanes),
            jax.ShapeDtypeStruct((half, columns, 2 * bins), BF16),
            jax.ShapeDtypeStruct((2, half, columns // 2, 2 * bins), BF16),
        ],
        [
            strip_spec(channels),
            strip_spec(lanes),
            by_row_spec,
            pl.BlockSpec((2, ROWS, columns // 2, 2 * bins), lambda step: (0, step, 0, 0)),
        ],
        scratch(far),
        cost(1, 14),
        "head",
    )
    facing = facing_logits(by_column.reshape(rows, columns // 2, 2 * bins))

    own_labels = lax.all_to_all(labels, "col", split_axis=1, concat_axis=0, tiled=True)
    facing_labels = facing_tile(own_labels).T
    numbers = jnp.arange(bins, dtype=jnp.int32)

    def onehot(values):
        return (values[:, :, None] == numbers).astype(F32)

    targets = jnp.concatenate(
        [
            0.5 * (onehot(own_labels[part]) + onehot(facing_labels[part]))
            for part in (slice(0, half), slice(half, rows))
        ],
        axis=2,
    ).astype(BF16)

    inner = 16 // ROWS
    grad_2, conv_grad_2, *sent = call(
        functools.partial(loss_kernel, far, steps),
        (by_row, facing, targets, stream_2, activated_2, gains[2], head_back, group, ups_back[1]),
        [
            by_row_spec,
            pl.BlockSpec((columns, ROWS * inner, 2 * bins), lambda step: (0, step // inner, 0)),
            by_row_spec,
            bf_spec,
            strip_spec(lanes),
        ]
        + [whole(array) for array in (gains[2], head_back, group, ups_back[1])],
        [halves(F32, channels), halves(BF16, lanes)] + far_shapes,
        [strip_spec(channels), strip_spec(lanes)] + far_specs,
        [pltpu.VMEM((ROWS * inner, columns, 2 * bins), F32)],
        cost(0, 18),
        "loss",
    )
    halos = exchange(sent)

    centre = tile(conv_grad_2)
    grad_1, conv_grad_1, *sent = call(
        functools.partial(back_kernel, far, near, steps),
        (centre, *halos, convs_back[1], squeezed_2, downs_back[1], stream_1, gains[1], grad_2, activated_1, ups_back[0]),
        [whole(centre)] + [whole(halo) for halo in halos]
        + [
            whole(convs_back[1]),
            strip_spec(lanes),
            whole(downs_back[1]),
            bf_spec,
            whole(gains[1]),
            bf_spec,
            strip_spec(lanes),
            whole(ups_back[0]),
        ],
        [halves(F32, channels), halves(BF16, lanes)] + near_shapes,
        [strip_spec(channels), strip_spec(lanes)] + near_specs,
        scratch(far),
        cost(1, 20),
        "back",
    )
    halos = exchange(sent)

    centre = tile(conv_grad_1)
    (grad_0,) = call(
        functools.partial(final_kernel, near),
        (centre, *halos, convs_back[0], squeezed_1, downs_back[0], split, gains[0], grad_1),
        [whole(centre)] + [whole(halo) for halo in halos]
        + [
            whole(convs_back[0]),
            strip_spec(lanes),
            whole(downs_back[0]),
            bf_spec,
            whole(gains[0]),
            bf_spec,
        ],
        [halves(F32, channels)],
        [strip_spec(channels)],
        scratch(near),
        cost(1, 16),
        "final",
    )
    return grad_0.reshape(features.shape)


def solution(mesh):
    return jax.shard_map(
        shards,
        mesh=mesh,
        in_specs=(
            P(("dp", "row"), "col", None),
            P(("dp", "row", "col"), None),
            P(),
            P(),
            P(),
            P(),
            P(),
            P(),
        ),
        out_specs=P(("dp", "row"), "col", None),
        check_vma=False,
    )
```

```python
import functools
import math

import jax
import jax.numpy as jnp
from jax import lax
from jax.experimental import pallas as pl
from jax.experimental.pallas import tpu as pltpu
from jax.sharding import PartitionSpec as P

epsilon = 1e-05
F32 = jnp.float32
BF16 = jnp.bfloat16
ROWS = 4
EDGE = 8
PAD = 16


def lane_low(shape):
    return lax.broadcasted_iota(jnp.int32, shape, len(shape) - 1) < shape[-1] // 2


def standardize(values):
    count = values.shape[-1]
    centred = values - jnp.sum(values, -1, keepdims=True) * (1.0 / count)
    inverse = lax.rsqrt(jnp.sum(centred * centred, -1, keepdims=True) + epsilon * count)
    return centred * inverse, inverse


def elu(values):
    return jnp.maximum(values, jnp.exp(jnp.minimum(values, 0.0)) - 1.0)


def slope_from_elu(activated):
    return 1.0 + jnp.minimum(activated, 0.0)


def standardize_back(standard, inverse, upstream):
    along = jnp.sum(upstream, -1, keepdims=True) * (1.0 / upstream.shape[-1])
    across = jnp.sum(upstream * standard, -1, keepdims=True)
    return inverse * (upstream - along - standard * across)


def squeeze(stream, gain, down):
    standard, unused = standardize(stream)
    entered = elu(standard * gain).astype(BF16)
    return elu(jnp.dot(entered, down, preferred_element_type=F32))


def store_edges(values, refs, spacing, step, steps):
    top, bottom, left, right = refs
    columns = values.shape[2]
    low = lane_low((ROWS, EDGE, values.shape[3]))
    left[...] = jnp.where(low, values[0, :, :EDGE], values[1, :, :EDGE]).astype(BF16)
    right[...] = jnp.where(low, values[0, :, columns - EDGE :], values[1, :, columns - EDGE :]).astype(BF16)
    wide = lane_low((ROWS, columns // 2, values.shape[3]))
    taken = spacing // ROWS

    @pl.when(step < taken)
    def _():
        top[...] = jnp.where(wide, values[0, :, : columns // 2], values[0, :, columns // 2 :]).astype(BF16)

    @pl.when(step >= steps - taken)
    def _():
        bottom[...] = jnp.where(wide, values[1, :, : columns // 2], values[1, :, columns // 2 :]).astype(BF16)


def fill_padded(padded, centre, halos, spacing):
    above, below, before, after = halos
    rows, columns, lanes = centre.shape
    half = rows // 2

    def lay(row, carry):
        padded[spacing + row, PAD : PAD + columns] = centre[row]
        return carry

    lax.fori_loop(0, rows, lay, 0)

    def twice(packed):
        turned = pltpu.roll(packed, lanes // 2, packed.ndim - 1)
        low = lane_low(packed.shape)
        return jnp.where(low, packed, turned).astype(BF16), jnp.where(low, turned, packed).astype(BF16)

    def sides(row, carry):
        for halo, start in ((before, PAD - EDGE), (after, PAD + columns)):
            first, second = twice(halo[row].astype(F32))
            padded[spacing + row, start : start + EDGE] = first
            padded[spacing + half + row, start : start + EDGE] = second
        return carry

    lax.fori_loop(0, half, sides, 0)
    for halo, base, place in ((above, 0, half), (below, spacing + rows, half + spacing)):
        for row in range(spacing):
            first, second = twice(halo[row].astype(F32))
            padded[base + row, PAD : PAD + columns // 2] = first
            padded[base + row, PAD + columns // 2 : PAD + columns] = second
            padded[base + row, PAD - EDGE : PAD] = twice(before[place + row].astype(F32))[1]
            padded[base + row, PAD + columns : PAD + columns + EDGE] = twice(after[place + row].astype(F32))[0]


def convolve(padded, kernel, taps, spacing, step, half, columns):
    width = columns + 2 * PAD
    lanes = padded.shape[2]
    low = lane_low((ROWS, width, lanes))
    parts = []
    for side in range(2):
        start = side * half + step * ROWS
        first, second, third = (padded[pl.ds(start + tap * spacing, ROWS)] for tap in range(3))
        parts.append(jnp.concatenate([jnp.where(low, first, second), third], axis=2))
    joined = jnp.concatenate(parts, axis=0).reshape(2 * ROWS * width, 2 * lanes)
    taps[...] = jnp.dot(joined, kernel[...], preferred_element_type=F32).reshape(2 * ROWS, width, 3 * lanes)
    total = taps[:, PAD : PAD + columns, lanes : 2 * lanes]
    if spacing % EDGE:
        outer = taps[:, PAD - EDGE : PAD + columns, :lanes]
        start = PAD - EDGE + 2 * spacing
        outer = outer + taps[:, start : start + columns + EDGE, 2 * lanes :]
        total = total + outer[:, EDGE - spacing : EDGE - spacing + columns]
    else:
        total = total + taps[:, PAD - spacing : PAD - spacing + columns, :lanes]
        total = total + taps[:, PAD + spacing : PAD + spacing + columns, 2 * lanes :]
    return total.reshape(2 * ROWS * columns, lanes)


def strip(reference):
    return reference[...].reshape(-1, reference.shape[-1])


def entry_kernel(spacing, steps, features, gain, down, squeezed, *edges):
    step = pl.program_id(0)
    values = squeeze(strip(features).astype(F32), gain[...], down[...]).reshape(squeezed.shape)
    squeezed[...] = values.astype(BF16)
    store_edges(values, edges, spacing, step, steps)


def middle_kernel(near, far, steps, centre, *rest):
    halos, rest = rest[:4], rest[4:]
    features, kernel, up, gain, down, stream_out, activated_out, squeezed, *rest = rest
    edges, (padded, taps) = rest[:4], rest[4:]
    step = pl.program_id(0)
    half, columns = centre.shape[0] // 2, centre.shape[1]

    @pl.when(step == 0)
    def _():
        fill_padded(padded, centre, halos, near)

    activated = elu(convolve(padded, kernel, taps, near, step, half, columns)).astype(BF16)
    activated_out[...] = activated.reshape(activated_out.shape)
    stream = strip(features).astype(F32) + jnp.dot(activated, up[...], preferred_element_type=F32)
    stream_out[...] = stream.reshape(stream_out.shape)
    values = squeeze(stream, gain[...], down[...]).reshape(squeezed.shape)
    squeezed[...] = values.astype(BF16)
    store_edges(values, edges, far, step, steps)


def head_kernel(near, steps, centre, *rest):
    halos, rest = rest[:4], rest[4:]
    stream_in, kernel, up, gain, head, bias, stream_out, activated_out, by_row, by_column, padded, taps = rest
    step = pl.program_id(0)
    half, columns = centre.shape[0] // 2, centre.shape[1]

    @pl.when(step == 0)
    def _():
        fill_padded(padded, centre, halos, near)

    activated = elu(convolve(padded, kernel, taps, near, step, half, columns)).astype(BF16)
    activated_out[...] = activated.reshape(activated_out.shape)
    stream = strip(stream_in) + jnp.dot(activated, up[...], preferred_element_type=F32)
    stream_out[...] = stream.reshape(stream_out.shape)
    standard, unused = standardize(stream)
    entered = (standard * gain[...]).astype(BF16).reshape(2, ROWS, columns, stream.shape[1])
    pairs = jnp.concatenate([entered[0], entered[1]], axis=2).reshape(ROWS * columns, -1)
    logits = jnp.dot(pairs, head[...], preferred_element_type=F32) + bias[...]
    by_row[...] = logits.astype(BF16).reshape(by_row.shape)
    pairs = jnp.concatenate([entered[:, :, : columns // 2], entered[:, :, columns // 2 :]], axis=3)
    logits = jnp.dot(pairs.reshape(ROWS * columns, -1), head[...], preferred_element_type=F32) + bias[...]
    by_column[...] = logits.astype(BF16).reshape(by_column.shape)


def loss_kernel(
    spacing, steps, inner, pieces, by_row, *rest
):
    facing, rest = rest[: sum(pieces)], rest[sum(pieces) :]
    targets, stream, activated, gain, head, group, up, grad_out, conv_out, *rest = rest
    edges, (turned,) = rest[:4], rest[4:]
    step = pl.program_id(0)

    @pl.when(step % inner == 0)
    def _():
        place = taken = 0
        for count in pieces:
            piece = sum(array[...].astype(F32) for array in facing[taken : taken + count])
            turned[:, place : place + piece.shape[0]] = jnp.swapaxes(piece, 0, 1)
            place, taken = place + piece.shape[0], taken + count

    start = (step % inner) * ROWS
    columns, lanes = by_row.shape[1:]
    symmetric = 0.5 * (by_row[...].astype(F32) + turned[pl.ds(start, ROWS)])
    exponent = jnp.exp(symmetric).reshape(ROWS * columns, lanes)
    upper = exponent.astype(BF16)
    lower = (exponent - upper.astype(F32)).astype(BF16)
    total = jnp.dot(upper, group[...], preferred_element_type=F32) + jnp.dot(
        lower, group[...], preferred_element_type=F32
    )
    logit_grad = (exponent / total - targets[...].astype(F32).reshape(exponent.shape)).astype(BF16)
    back = jnp.dot(logit_grad, head[...], preferred_element_type=F32)
    width = back.shape[1] // 2
    back = jnp.concatenate([back[:, :width], back[:, width:]], axis=0)
    standard, inverse = standardize(strip(stream))
    grad = standardize_back(standard, inverse, back * gain[...])
    grad_out[...] = grad.reshape(grad_out.shape)
    values = jnp.dot(grad.astype(BF16), up[...], preferred_element_type=F32)
    values = values * slope_from_elu(strip(activated).astype(F32))
    values = values.reshape(conv_out.shape)
    conv_out[...] = values.astype(BF16)
    store_edges(values, edges, spacing, step, steps)


def back_strip(spacing, step, centre, padded, taps, kernel, squeezed, down, stream, gain, upstream):
    half, columns = centre.shape[0] // 2, centre.shape[1]
    lowered = convolve(padded, kernel, taps, spacing, step, half, columns)
    lowered = lowered * slope_from_elu(strip(squeezed).astype(F32))
    entered = jnp.dot(lowered.astype(BF16), down[...], preferred_element_type=F32)
    standard, inverse = standardize(strip(stream).astype(F32))
    scale = gain[...]
    entered = entered * (jnp.exp2(jnp.minimum(standard * (scale * math.log2(math.e)), 0.0)) * scale)
    return strip(upstream) + standardize_back(standard, inverse, entered)


def back_kernel(near, far, steps, centre, *rest):
    halos, rest = rest[:4], rest[4:]
    kernel, squeezed, down, stream, gain, upstream, activated, up, grad_out, conv_out, *rest = rest
    edges, (padded, taps) = rest[:4], rest[4:]
    step = pl.program_id(0)

    @pl.when(step == 0)
    def _():
        fill_padded(padded, centre, halos, near)

    grad = back_strip(near, step, centre, padded, taps, kernel, squeezed, down, stream, gain, upstream)
    grad_out[...] = grad.reshape(grad_out.shape)
    values = jnp.dot(grad.astype(BF16), up[...], preferred_element_type=F32)
    values = values * slope_from_elu(strip(activated).astype(F32))
    values = values.reshape(conv_out.shape)
    conv_out[...] = values.astype(BF16)
    store_edges(values, edges, far, step, steps)


def final_kernel(near, centre, *rest):
    halos, rest = rest[:4], rest[4:]
    kernel, squeezed, down, stream, gain, upstream, grad_out, padded, taps = rest
    step = pl.program_id(0)

    @pl.when(step == 0)
    def _():
        fill_padded(padded, centre, halos, near)

    grad = back_strip(near, step, centre, padded, taps, kernel, squeezed, down, stream, gain, upstream)
    grad_out[...] = grad.reshape(grad_out.shape)


def shifted(values, axis, move):
    count = lax.axis_size(axis)
    return lax.ppermute(values, axis, [(i, i + move) for i in range(count) if 0 <= i + move < count])


def exchange(edges):
    top, bottom, left, right = edges
    above = shifted(bottom, "row", 1)
    below = shifted(top, "row", -1)
    before = jnp.concatenate([right, above[:, -EDGE:], below[:, -EDGE:]], axis=0)
    after = jnp.concatenate([left, above[:, :EDGE], below[:, :EDGE]], axis=0)
    return above, below, shifted(before, "col", 1), shifted(after, "col", -1)


def facing_tile(tile):
    rows, cols = lax.axis_size("row"), lax.axis_size("col")
    if rows == cols:
        pairs = [(row * cols + col, col * cols + row) for row in range(rows) for col in range(cols)]
        return lax.ppermute(tile, ("row", "col"), pairs)
    if cols % rows:
        raise ValueError("unsupported mesh")
    times = cols // rows
    height = tile.shape[0] // times
    place = lax.axis_index("col") % times
    received = []
    for turn in range(times):
        piece = lax.dynamic_slice_in_dim(tile, ((place + turn) % times) * height, height, axis=0)
        pairs = [
            (row * cols + col, (col // times) * cols + times * row + (col % times + turn) % times)
            for row in range(rows)
            for col in range(cols)
        ]
        received.append(lax.ppermute(piece, ("row", "col"), pairs))
    stacked = jnp.stack(received)
    pieces = [
        lax.dynamic_index_in_dim(stacked, (place - source) % times, axis=0, keepdims=False)
        for source in range(times)
    ]
    return jnp.concatenate(pieces, axis=1)


def facing_logits(by_column):
    rows, cols = lax.axis_size("row"), lax.axis_size("col")
    if rows == cols and rows % 2 == 0:
        cut = by_column.shape[0] * 5 // 128 * 16
        straight, around = by_column[:cut], by_column[cut:]
        places = [(row, col) for row in range(rows) for col in range(cols)]
        part = rows // 2
        far = [(row, col) for row, col in places if row // part != col // part]
        close = [(row, col) for row, col in places if row // part == col // part]
        both = ("row", "col")
        number = lambda row, col: row * cols + col
        other = lambda row: (row + part) % rows
        hop = lax.ppermute(around, both, [(number(row, col), number(other(row), col)) for row, col in far])
        straight = lax.ppermute(straight, both, [(number(row, col), number(col, row)) for row, col in places])
        near = lax.ppermute(around, both, [(number(row, col), number(col, row)) for row, col in close])
        hop = lax.ppermute(hop, both, [(number(other(row), col), number(col, row)) for row, col in far])
        return [[straight], [hop, near]]
    if rows == cols:
        return [[facing_tile(by_column)]]
    bins = by_column.shape[2] // 2
    tile = facing_tile(jnp.concatenate([by_column[..., :bins], by_column[..., bins:]], axis=1))
    half = tile.shape[1] // 2
    return [[jnp.concatenate([tile[:, :half], tile[:, half:]], axis=2)]]


def dilated_weights(kernel):
    twice = jnp.concatenate([kernel, kernel], axis=3)
    flat = jnp.transpose(twice, (0, 2, 1, 3)).reshape(3 * kernel.shape[2], -1)
    return jnp.pad(flat, ((0, kernel.shape[2]), (0, 0)))


def mirrored(kernel):
    return jnp.swapaxes(kernel[::-1, ::-1], 2, 3)


def doubled_columns(weight):
    return jnp.concatenate([weight, weight], axis=1)


def padded_rows(weight):
    return jnp.pad(weight, ((0, weight.shape[0]), (0, 0)))


def diagonal(weight):
    zeros = jnp.zeros_like(weight)
    return jnp.concatenate(
        [jnp.concatenate([weight, zeros], axis=1), jnp.concatenate([zeros, weight], axis=1)], axis=0
    )


def shards(features, labels, norm_gain, w_down, w_conv, w_up, w_head, head_bias):
    rows, columns, channels = features.shape
    narrow = w_down.shape[2]
    bins = w_head.shape[1]
    half = rows // 2
    steps = half // ROWS
    lanes = 2 * narrow
    near, far = 4, 8

    gains = [norm_gain[index : index + 1] * math.sqrt(channels) for index in range(3)]
    downs = [doubled_columns(w_down[index]) for index in range(2)]
    downs_back = [padded_rows(w_down[index].T) for index in range(2)]
    ups = [padded_rows(w_up[index]) for index in range(2)]
    ups_back = [doubled_columns(w_up[index].T) for index in range(2)]
    convs = [dilated_weights(w_conv[index]) for index in range(2)]
    convs_back = [dilated_weights(mirrored(w_conv[index])) for index in range(2)]
    head = diagonal(w_head)
    head_back = diagonal(w_head.T)
    bias = jnp.concatenate([head_bias, head_bias])[None]
    group = diagonal(jnp.ones((bins, bins), BF16))

    def whole(array):
        zeros = (0,) * array.ndim
        return pl.BlockSpec(array.shape, lambda step: zeros)

    def strip_spec(width):
        return pl.BlockSpec((2, ROWS, columns, width), lambda step: (0, step, 0, 0))

    def halves(dtype, width):
        return jax.ShapeDtypeStruct((2, half, columns, width), dtype)

    def edges(spacing):
        taken = spacing // ROWS
        first = lambda step: (jnp.minimum(step, taken - 1), 0, 0)
        last = lambda step: (jnp.maximum(step - (steps - taken), 0), 0, 0)
        each = lambda step: (step, 0, 0)
        entries = [
            ((spacing, columns // 2, lanes), first),
            ((spacing, columns // 2, lanes), last),
            ((half, EDGE, lanes), each),
            ((half, EDGE, lanes), each),
        ]
        shapes = [jax.ShapeDtypeStruct(shape, BF16) for shape, index in entries]
        specs = [pl.BlockSpec((ROWS,) + shape[1:], index) for shape, index in entries]
        return shapes, specs

    def scratch(spacing):
        width = columns + 2 * PAD
        return [
            pltpu.VMEM((rows + 2 * spacing, width, lanes), BF16),
            pltpu.VMEM((2 * ROWS, width, 3 * lanes), F32),
        ]

    def cost(convolutions, passes):
        pixels = rows * columns
        return pl.CostEstimate(
            flops=pixels * (convolutions * 18 * narrow * narrow + 4 * narrow * channels),
            bytes_accessed=pixels * channels * passes,
            transcendentals=pixels * channels,
        )

    def call(body, inputs, specs, shapes, out_specs, scratch_shapes, estimate, name):
        return pl.pallas_call(
            body,
            grid=(steps,),
            in_specs=specs,
            out_specs=out_specs,
            out_shape=shapes,
            scratch_shapes=scratch_shapes,
            compiler_params=pltpu.CompilerParams(vmem_limit_bytes=56 * 1024 * 1024),
            cost_estimate=estimate,
            name=name,
        )(*inputs)

    split = features.reshape(2, half, columns, channels)
    bf_spec = strip_spec(channels)
    near_shapes, near_specs = edges(near)
    far_shapes, far_specs = edges(far)

    squeezed_1, *sent = call(
        functools.partial(entry_kernel, near, steps),
        (split, gains[0], downs[0]),
        [bf_spec, whole(gains[0]), whole(downs[0])],
        [halves(BF16, lanes)] + near_shapes,
        [strip_spec(lanes)] + near_specs,
        [],
        cost(0, 4),
        "entry",
    )
    own_labels = lax.all_to_all(labels, "col", split_axis=1, concat_axis=0, tiled=True)
    squeezed_1, own_labels = lax.optimization_barrier((squeezed_1, own_labels))
    halos = exchange(sent)

    def tile(array):
        return array.reshape(rows, columns, array.shape[-1])

    centre = tile(squeezed_1)
    stream_1, activated_1, squeezed_2, *sent = call(
        functools.partial(middle_kernel, near, far, steps),
        (centre, *halos, split, convs[0], ups[0], gains[1], downs[1]),
        [whole(centre)] + [whole(halo) for halo in halos] + [bf_spec]
        + [whole(array) for array in (convs[0], ups[0], gains[1], downs[1])],
        [halves(F32, channels), halves(BF16, lanes), halves(BF16, lanes)] + far_shapes,
        [strip_spec(channels), strip_spec(lanes), strip_spec(lanes)] + far_specs,
        scratch(near),
        cost(1, 12),
        "middle",
    )
    halos = exchange(sent)

    facing_labels = facing_tile(own_labels)
    squeezed_2, facing_labels = lax.optimization_barrier((squeezed_2, facing_labels))
    facing_labels = facing_labels.T
    centre = tile(squeezed_2)
    by_row_spec = pl.BlockSpec((ROWS, columns, 2 * bins), lambda step: (step, 0, 0))
    stream_2, activated_2, by_row, by_column = call(
        functools.partial(head_kernel, far, steps),
        (centre, *halos, stream_1, convs[1], ups[1], gains[2], head, bias),
        [whole(centre)] + [whole(halo) for halo in halos] + [bf_spec]
        + [whole(array) for array in (convs[1], ups[1], gains[2], head, bias)],
        [
            halves(F32, channels),
            halves(BF16, lanes),
            jax.ShapeDtypeStruct((half, columns, 2 * bins), BF16),
            jax.ShapeDtypeStruct((2, half, columns // 2, 2 * bins), BF16),
        ],
        [
            strip_spec(channels),
            strip_spec(lanes),
            by_row_spec,
            pl.BlockSpec((2, ROWS, columns // 2, 2 * bins), lambda step: (0, step, 0, 0)),
        ],
        scratch(far),
        cost(1, 14),
        "head",
    )
    facing = facing_logits(by_column.reshape(rows, columns // 2, 2 * bins))

    numbers = jnp.arange(bins, dtype=jnp.int32)

    def onehot(values):
        return (values[:, :, None] == numbers).astype(F32)

    targets = jnp.concatenate(
        [
            0.5 * (onehot(own_labels[part]) + onehot(facing_labels[part]))
            for part in (slice(0, half), slice(half, rows))
        ],
        axis=2,
    ).astype(BF16)

    inner = 16 // ROWS
    mirrored_logits = [array for piece in facing for array in piece]
    grad_2, conv_grad_2, *sent = call(
        functools.partial(loss_kernel, far, steps, inner, tuple(len(piece) for piece in facing)),
        (by_row, *mirrored_logits, targets, stream_2, activated_2, gains[2], head_back, group, ups_back[1]),
        [
            by_row_spec,
            *(pl.BlockSpec((array.shape[0], ROWS * inner, 2 * bins), lambda step: (0, step // inner, 0))
              for array in mirrored_logits),
            by_row_spec,
            bf_spec,
            strip_spec(lanes),
        ]
        + [whole(array) for array in (gains[2], head_back, group, ups_back[1])],
        [halves(F32, channels), halves(BF16, lanes)] + far_shapes,
        [strip_spec(channels), strip_spec(lanes)] + far_specs,
        [pltpu.VMEM((ROWS * inner, columns, 2 * bins), F32)],
        cost(0, 18),
        "loss",
    )
    halos = exchange(sent)

    centre = tile(conv_grad_2)
    grad_1, conv_grad_1, *sent = call(
        functools.partial(back_kernel, far, near, steps),
        (centre, *halos, convs_back[1], squeezed_2, downs_back[1], stream_1, gains[1], grad_2, activated_1, ups_back[0]),
        [whole(centre)] + [whole(halo) for halo in halos]
        + [
            whole(convs_back[1]),
            strip_spec(lanes),
            whole(downs_back[1]),
            bf_spec,
            whole(gains[1]),
            bf_spec,
            strip_spec(lanes),
            whole(ups_back[0]),
        ],
        [halves(F32, channels), halves(BF16, lanes)] + near_shapes,
        [strip_spec(channels), strip_spec(lanes)] + near_specs,
        scratch(far),
        cost(1, 20),
        "back",
    )
    halos = exchange(sent)

    centre = tile(conv_grad_1)
    (grad_0,) = call(
        functools.partial(final_kernel, near),
        (centre, *halos, convs_back[0], squeezed_1, downs_back[0], split, gains[0], grad_1),
        [whole(centre)] + [whole(halo) for halo in halos]
        + [
            whole(convs_back[0]),
            strip_spec(lanes),
            whole(downs_back[0]),
            bf_spec,
            whole(gains[0]),
            bf_spec,
        ],
        [halves(F32, channels)],
        [strip_spec(channels)],
        scratch(near),
        cost(1, 16),
        "final",
    )
    return grad_0.reshape(features.shape)


def solution(mesh):
    return jax.shard_map(
        shards,
        mesh=mesh,
        in_specs=(
            P(("dp", "row"), "col", None),
            P(("dp", "row", "col"), None),
            P(),
            P(),
            P(),
            P(),
            P(),
            P(),
        ),
        out_specs=P(("dp", "row"), "col", None),
        check_vma=False,
    )
```

```python
import functools
import math

import jax
import jax.numpy as jnp
from jax import lax
from jax.experimental import pallas as pl
from jax.experimental.pallas import tpu as pltpu
from jax.sharding import PartitionSpec as P

epsilon = 1e-05
F32 = jnp.float32
BF16 = jnp.bfloat16
BLOCK = 16
ROWS = 16
EDGE = 8
PAD = 16


def lane_low(shape):
    return lax.broadcasted_iota(jnp.int32, shape, len(shape) - 1) < shape[-1] // 2


def lane_sums(values, ones):
    return jnp.sum(values, -1, keepdims=True)


def standardize(centred, ones):
    inverse = lax.rsqrt(lane_sums(centred * centred, ones) + epsilon * centred.shape[-1])
    return centred * inverse, inverse


def elu(values):
    return jnp.maximum(values, jnp.exp(jnp.minimum(values, 0.0)) - 1.0)


def slope_from_elu(activated):
    return 1.0 + jnp.minimum(activated, 0.0)


def standardize_back(standard, inverse, upstream, ones):
    return inverse * (upstream - standard * lane_sums(upstream * standard, ones))


def side_by_side(values):
    count = values.shape[0] // 2
    return jnp.concatenate([values[:count], values[count:]], axis=1)


def stacked(values):
    width = values.shape[1] // 2
    return jnp.concatenate([values[:, :width], values[:, width:]], axis=0)


def swapped(values):
    flat = values.reshape(-1, values.shape[-1])
    return pltpu.roll(flat, flat.shape[1] // 2, 1).reshape(values.shape)


def squeeze(centred, ones, gain, down):
    standard, unused = standardize(centred, ones)
    entered = elu(standard * gain).astype(BF16)
    return elu(jnp.dot(side_by_side(entered), down, preferred_element_type=F32))


def widened(activated, weight):
    return stacked(jnp.dot(jnp.concatenate([activated, activated], axis=1), weight, preferred_element_type=F32))


def store_edges(values, refs, spacing, step, steps):
    top, bottom, left, right = refs
    middle = values.shape[1] // 2
    left[...] = values[:, :EDGE].astype(BF16)
    right[...] = values[:, values.shape[1] - EDGE :].astype(BF16)
    count = min(ROWS, spacing)
    low = lane_low((count, middle, values.shape[2]))
    taken = spacing // count

    @pl.when(step < taken)
    def _():
        sent = values[:count]
        rows = pl.ds(jnp.minimum(step, taken - 1) * count, count)
        top[rows] = jnp.where(low, sent[:, :middle], swapped(sent[:, middle:])).astype(BF16)

    @pl.when(step >= steps - taken)
    def _():
        sent = values[ROWS - count :]
        rows = pl.ds(jnp.maximum(step - (steps - taken), 0) * count, count)
        bottom[rows] = jnp.where(low, swapped(sent[:, :middle]), sent[:, middle:]).astype(BF16)


def fill_padded(padded, centre, halos, spacing):
    above, below, before, after = halos
    half, columns, lanes = centre.shape
    middle = columns // 2

    def lay(row, carry):
        padded[spacing + row, PAD : PAD + columns] = centre[row]
        padded[spacing + row, PAD - EDGE : PAD] = before[row]
        padded[spacing + row, PAD + columns : PAD + columns + EDGE] = after[row]
        return carry

    lax.fori_loop(0, half, lay, 0)
    wide, slim = lane_low((middle, lanes)), lane_low((EDGE, lanes))

    def put(row, start, low, first, second):
        padded[row, start : start + low.shape[0]] = jnp.where(low, first, second).astype(BF16)

    def read(array, row):
        return array[row].astype(F32)

    for row in range(spacing):
        own = swapped(read(centre, half - spacing + row))
        sent = read(above, row)
        put(row, PAD, wide, sent, own[:middle])
        put(row, PAD + middle, wide, swapped(sent), own[middle:])
        edge = half - spacing + row
        put(row, PAD - EDGE, slim, swapped(read(before, half + row)), swapped(read(before, edge)))
        put(row, PAD + columns, slim, read(after, half + row), swapped(read(after, edge)))
        place = spacing + half + row
        own = swapped(read(centre, row))
        sent = read(below, row)
        put(place, PAD, wide, own[:middle], swapped(sent))
        put(place, PAD + middle, wide, own[middle:], sent)
        corner = half + spacing + row
        put(place, PAD - EDGE, slim, swapped(read(before, row)), read(before, corner))
        put(place, PAD + columns, slim, swapped(read(after, row)), swapped(read(after, corner)))


def convolve(padded, kernel, taps, spacing, step, columns):
    width = columns + 2 * PAD
    lanes = padded.shape[2]
    parts = [padded[pl.ds(step * ROWS + tap * spacing, ROWS)] for tap in range(3)]
    joined = jnp.concatenate(parts, axis=2).reshape(ROWS * width, 3 * lanes)
    taps[...] = jnp.dot(joined, kernel[...], preferred_element_type=F32).reshape(ROWS, width, 3 * lanes)
    total = taps[:, PAD : PAD + columns, lanes : 2 * lanes]
    if spacing % EDGE:
        outer = taps[:, PAD - EDGE : PAD + columns, :lanes]
        start = PAD - EDGE + 2 * spacing
        outer = outer + taps[:, start : start + columns + EDGE, 2 * lanes :]
        total = total + outer[:, EDGE - spacing : EDGE - spacing + columns]
    else:
        total = total + taps[:, PAD - spacing : PAD - spacing + columns, :lanes]
        total = total + taps[:, PAD + spacing : PAD + spacing + columns, 2 * lanes :]
    return total.reshape(ROWS * columns, lanes)


def strip(reference):
    return reference[...].reshape(-1, reference.shape[-1])


def over_strips(body, kinds, *refs):
    inner = BLOCK // ROWS

    def one(place, carry):
        rows = pl.ds(place * ROWS, ROWS)
        views = []
        for kind, ref in zip(kinds, refs):
            views.append(ref.at[:, rows] if kind == "halves" else ref.at[rows] if kind == "rows" else ref)
        body(pl.program_id(0) * inner + place, *views)
        return carry

    lax.fori_loop(0, inner, one, 0)


def entry_kernel(spacing, steps, step, features, centring, ones, gain, down, squeezed, *edges):
    centred = jnp.dot(strip(features), centring[...], preferred_element_type=F32)
    values = squeeze(centred, ones, gain[...], down[...]).reshape(squeezed.shape)
    squeezed[...] = values.astype(BF16)
    store_edges(values, edges, spacing, step, steps)


def middle_kernel(near, far, steps, step, centre, *rest):
    halos, rest = rest[:4], rest[4:]
    features, centring, ones, kernel, up, gain, down, stream_out, activated_out, squeezed, *rest = rest
    edges, (padded, taps) = rest[:4], rest[4:]
    columns = centre.shape[1]

    @pl.when(step == 0)
    def _():
        fill_padded(padded, centre, halos, near)

    activated = elu(convolve(padded, kernel, taps, near, step, columns)).astype(BF16)
    activated_out[...] = activated.reshape(activated_out.shape)
    stream = jnp.dot(strip(features), centring[...], preferred_element_type=F32) + widened(activated, up[...])
    stream_out[...] = stream.reshape(stream_out.shape)
    values = squeeze(stream, ones, gain[...], down[...]).reshape(squeezed.shape)
    squeezed[...] = values.astype(BF16)
    store_edges(values, edges, far, step, steps)


def head_kernel(near, steps, step, centre, *rest):
    halos, rest = rest[:4], rest[4:]
    stream_in, ones, kernel, up, gain, head, bias, stream_out, activated_out, by_row, by_column, padded, taps = rest
    columns = centre.shape[1]

    @pl.when(step == 0)
    def _():
        fill_padded(padded, centre, halos, near)

    activated = elu(convolve(padded, kernel, taps, near, step, columns)).astype(BF16)
    activated_out[...] = activated.reshape(activated_out.shape)
    stream = strip(stream_in) + widened(activated, up[...])
    stream_out[...] = stream.reshape(stream_out.shape)
    standard, unused = standardize(stream, ones)
    entered = (standard * gain[...]).astype(BF16).reshape(2, ROWS, columns, stream.shape[1])
    pairs = jnp.concatenate([entered[0], entered[1]], axis=2).reshape(ROWS * columns, -1)
    logits = jnp.dot(pairs, head[...], preferred_element_type=F32) + bias[...]
    by_row[...] = logits.astype(BF16).reshape(by_row.shape)
    pairs = jnp.concatenate([entered[:, :, : columns // 2], entered[:, :, columns // 2 :]], axis=3)
    logits = jnp.dot(pairs.reshape(ROWS * columns, -1), head[...], preferred_element_type=F32) + bias[...]
    by_column[...] = logits.astype(BF16).reshape(by_column.shape)


def loss_kernel(
    spacing, steps, inner, pieces, step, by_row, *rest
):
    facing, rest = rest[: sum(pieces)], rest[sum(pieces) :]
    targets, stream, activated, ones, head, group, up, grad_out, conv_out, *rest = rest
    edges, (turned,) = rest[:4], rest[4:]

    @pl.when(step % inner == 0)
    def _():
        place = taken = 0
        for count in pieces:
            piece = sum(array[...].astype(F32) for array in facing[taken : taken + count])
            turned[:, place : place + piece.shape[0]] = jnp.swapaxes(piece, 0, 1)
            place, taken = place + piece.shape[0], taken + count

    start = (step % inner) * ROWS
    columns, lanes = by_row.shape[1:]
    symmetric = 0.5 * (by_row[...].astype(F32) + turned[pl.ds(start, ROWS)])
    exponent = jnp.exp(symmetric).reshape(ROWS * columns, lanes)
    upper = exponent.astype(BF16)
    lower = (exponent - upper.astype(F32)).astype(BF16)
    total = jnp.dot(upper, group[...], preferred_element_type=F32) + jnp.dot(
        lower, group[...], preferred_element_type=F32
    )
    logit_grad = (exponent / total - targets[...].astype(F32).reshape(exponent.shape)).astype(BF16)
    back = widened(logit_grad, head[...])
    standard, inverse = standardize(strip(stream), ones)
    grad = standardize_back(standard, inverse, back, ones)
    grad_out[...] = grad.reshape(grad_out.shape)
    values = jnp.dot(side_by_side(grad.astype(BF16)), up[...], preferred_element_type=F32)
    values = values * slope_from_elu(strip(activated).astype(F32))
    values = values.reshape(conv_out.shape)
    conv_out[...] = values.astype(BF16)
    store_edges(values, edges, spacing, step, steps)


def back_strip(spacing, step, centre, padded, taps, kernel, squeezed, down, centred, ones, gain, upstream):
    columns = centre.shape[1]
    lowered = convolve(padded, kernel, taps, spacing, step, columns)
    lowered = lowered * slope_from_elu(strip(squeezed).astype(F32))
    entered = stacked(jnp.dot(lowered.astype(BF16), down[...], preferred_element_type=F32))
    standard, inverse = standardize(centred, ones)
    scale = gain[...]
    entered = entered * (jnp.exp2(jnp.minimum(standard * (scale * math.log2(math.e)), 0.0)) * scale)
    entered = entered - jnp.sum(entered, -1, keepdims=True) * (1.0 / entered.shape[-1])
    return strip(upstream) + standardize_back(standard, inverse, entered, ones)


def back_kernel(near, far, steps, step, centre, *rest):
    halos, rest = rest[:4], rest[4:]
    kernel, squeezed, down, stream, ones, gain, upstream, activated, up, grad_out, conv_out, *rest = rest
    edges, (padded, taps) = rest[:4], rest[4:]

    @pl.when(step == 0)
    def _():
        fill_padded(padded, centre, halos, near)

    grad = back_strip(near, step, centre, padded, taps, kernel, squeezed, down, strip(stream), ones, gain, upstream)
    grad_out[...] = grad.reshape(grad_out.shape)
    values = jnp.dot(side_by_side(grad.astype(BF16)), up[...], preferred_element_type=F32)
    values = values * slope_from_elu(strip(activated).astype(F32))
    values = values.reshape(conv_out.shape)
    conv_out[...] = values.astype(BF16)
    store_edges(values, edges, far, step, steps)


def final_kernel(near, step, centre, *rest):
    halos, rest = rest[:4], rest[4:]
    kernel, squeezed, down, features, centring, ones, gain, upstream, grad_out, padded, taps = rest

    @pl.when(step == 0)
    def _():
        fill_padded(padded, centre, halos, near)

    centred = jnp.dot(strip(features), centring[...], preferred_element_type=F32)
    grad = back_strip(near, step, centre, padded, taps, kernel, squeezed, down, centred, ones, gain, upstream)
    grad_out[...] = grad.reshape(grad_out.shape)


def shifted(values, axis, move):
    count = lax.axis_size(axis)
    return lax.ppermute(values, axis, [(i, i + move) for i in range(count) if 0 <= i + move < count])


def exchange(edges):
    top, bottom, left, right = edges
    above = shifted(bottom, "row", 1)
    below = shifted(top, "row", -1)
    before = jnp.concatenate([right, above[:, -EDGE:], below[:, -EDGE:]], axis=0)
    after = jnp.concatenate([left, above[:, :EDGE], below[:, :EDGE]], axis=0)
    return above, below, shifted(before, "col", 1), shifted(after, "col", -1)


def facing_tile(tile):
    rows, cols = lax.axis_size("row"), lax.axis_size("col")
    if rows == cols:
        pairs = [(row * cols + col, col * cols + row) for row in range(rows) for col in range(cols)]
        return lax.ppermute(tile, ("row", "col"), pairs)
    if cols % rows:
        raise ValueError("unsupported mesh")
    times = cols // rows
    height = tile.shape[0] // times
    place = lax.axis_index("col") % times
    received = []
    for turn in range(times):
        piece = lax.dynamic_slice_in_dim(tile, ((place + turn) % times) * height, height, axis=0)
        pairs = [
            (row * cols + col, (col // times) * cols + times * row + (col % times + turn) % times)
            for row in range(rows)
            for col in range(cols)
        ]
        received.append(lax.ppermute(piece, ("row", "col"), pairs))
    stacked = jnp.stack(received)
    pieces = [
        lax.dynamic_index_in_dim(stacked, (place - source) % times, axis=0, keepdims=False)
        for source in range(times)
    ]
    return jnp.concatenate(pieces, axis=1)


def facing_logits(by_column):
    rows, cols = lax.axis_size("row"), lax.axis_size("col")
    if rows == cols and rows % 2 == 0:
        cut = by_column.shape[0] * 5 // 128 * 16
        straight, around = by_column[:cut], by_column[cut:]
        places = [(row, col) for row in range(rows) for col in range(cols)]
        part = rows // 2
        far = [(row, col) for row, col in places if row // part != col // part]
        close = [(row, col) for row, col in places if row // part == col // part]
        both = ("row", "col")
        number = lambda row, col: row * cols + col
        other = lambda row: (row + part) % rows
        hop = lax.ppermute(around, both, [(number(row, col), number(other(row), col)) for row, col in far])
        straight = lax.ppermute(straight, both, [(number(row, col), number(col, row)) for row, col in places])
        near = lax.ppermute(around, both, [(number(row, col), number(col, row)) for row, col in close])
        hop = lax.ppermute(hop, both, [(number(other(row), col), number(col, row)) for row, col in far])
        return [[straight], [hop, near]]
    if rows == cols:
        return [[facing_tile(by_column)]]
    bins = by_column.shape[2] // 2
    tile = facing_tile(jnp.concatenate([by_column[..., :bins], by_column[..., bins:]], axis=1))
    half = tile.shape[1] // 2
    return [[jnp.concatenate([tile[:, :half], tile[:, half:]], axis=2)]]


def dilated_weights(kernel):
    both = jnp.eye(2, dtype=kernel.dtype)[None, :, None, None, :, None]
    spread = jnp.transpose(kernel, (0, 2, 1, 3))[:, None, :, :, None, :] * both
    return spread.reshape(6 * kernel.shape[2], 6 * kernel.shape[3])


def mirrored(kernel):
    return jnp.swapaxes(kernel[::-1, ::-1], 2, 3)


def diagonal(weight):
    zeros = jnp.zeros_like(weight)
    return jnp.concatenate(
        [jnp.concatenate([weight, zeros], axis=1), jnp.concatenate([zeros, weight], axis=1)], axis=0
    )


def two_parts(weight):
    centred = weight - jnp.mean(weight, axis=1, keepdims=True)
    upper = lax.reduce_precision(centred, 8, 7)
    return jnp.concatenate([diagonal(upper), diagonal(centred - upper)], axis=0).astype(BF16)


def shards(features, labels, norm_gain, w_down, w_conv, w_up, w_head, head_bias):
    rows, columns, channels = features.shape
    narrow = w_down.shape[2]
    bins = w_head.shape[1]
    half = rows // 2
    steps = half // ROWS
    lanes = 2 * narrow
    near, far = 4, 8

    gains = [norm_gain[index : index + 1] * math.sqrt(channels) for index in range(3)]
    downs = [diagonal(w_down[index]) for index in range(2)]
    downs_back = [diagonal(w_down[index].T) for index in range(2)]
    centring = (jnp.eye(channels) - 1.0 / channels).astype(BF16)
    ones = jnp.ones((channels, channels), BF16)
    ups = [two_parts(w_up[index].astype(F32)) for index in range(2)]
    ups_back = [diagonal(w_up[index].T) for index in range(2)]
    convs = [dilated_weights(w_conv[index]) for index in range(2)]
    convs_back = [dilated_weights(mirrored(w_conv[index])) for index in range(2)]
    head = diagonal(w_head)
    head_back = two_parts(w_head.T.astype(F32) * gains[2])
    bias = jnp.concatenate([head_bias, head_bias])[None]
    group = diagonal(jnp.ones((bins, bins), BF16))

    def whole(array):
        zeros = (0,) * len(array.shape)
        return "whole", pl.BlockSpec(array.shape, lambda step: zeros)

    def strip_spec(width):
        return "halves", pl.BlockSpec((2, BLOCK, columns, width), lambda step: (0, step, 0, 0))

    def halves(dtype, width):
        return jax.ShapeDtypeStruct((2, half, columns, width), dtype)

    pair_spec = "rows", pl.BlockSpec((BLOCK, columns, lanes), lambda step: (step, 0, 0))
    pair_shape = jax.ShapeDtypeStruct((half, columns, lanes), BF16)

    def edges(spacing):
        shapes = [jax.ShapeDtypeStruct((spacing, columns // 2, lanes), BF16)] * 2
        shapes += [jax.ShapeDtypeStruct((half, EDGE, lanes), BF16)] * 2
        sides = "rows", pl.BlockSpec((BLOCK, EDGE, lanes), lambda step: (step, 0, 0))
        return shapes, [whole(shapes[0]), whole(shapes[1]), sides, sides]

    def scratch(spacing):
        width = columns + 2 * PAD
        return [
            pltpu.VMEM((half + 2 * spacing, width, lanes), BF16),
            pltpu.VMEM((ROWS, width, 3 * lanes), F32),
        ]

    def cost(convolutions, passes):
        pixels = rows * columns
        return pl.CostEstimate(
            flops=pixels * (convolutions * 18 * narrow * narrow + 4 * narrow * channels),
            bytes_accessed=pixels * channels * passes,
            transcendentals=pixels * channels,
        )

    def call(body, inputs, specs, shapes, out_specs, scratch_shapes, estimate, name):
        kinds = [kind for kind, spec in specs + out_specs] + ["whole"] * len(scratch_shapes)
        return pl.pallas_call(
            functools.partial(over_strips, body, kinds),
            grid=(half // BLOCK,),
            in_specs=[spec for kind, spec in specs],
            out_specs=[spec for kind, spec in out_specs],
            out_shape=shapes,
            scratch_shapes=scratch_shapes,
            compiler_params=pltpu.CompilerParams(vmem_limit_bytes=56 * 1024 * 1024),
            cost_estimate=estimate,
            name=name,
        )(*inputs)

    split = features.reshape(2, half, columns, channels)
    bf_spec = strip_spec(channels)
    near_shapes, near_specs = edges(near)
    far_shapes, far_specs = edges(far)

    squeezed_1, *sent = call(
        functools.partial(entry_kernel, near, steps),
        (split, centring, ones, gains[0], downs[0]),
        [bf_spec] + [whole(array) for array in (centring, ones, gains[0], downs[0])],
        [pair_shape] + near_shapes,
        [pair_spec] + near_specs,
        [],
        cost(0, 4),
        "entry",
    )
    own_labels = lax.all_to_all(labels, "col", split_axis=1, concat_axis=0, tiled=True)
    squeezed_1, own_labels = lax.optimization_barrier((squeezed_1, own_labels))
    halos = exchange(sent)

    centre = squeezed_1
    stream_1, activated_1, squeezed_2, *sent = call(
        functools.partial(middle_kernel, near, far, steps),
        (centre, *halos, split, centring, ones, convs[0], ups[0], gains[1], downs[1]),
        [whole(centre)] + [whole(halo) for halo in halos] + [bf_spec]
        + [whole(array) for array in (centring, ones, convs[0], ups[0], gains[1], downs[1])],
        [halves(F32, channels), pair_shape, pair_shape] + far_shapes,
        [strip_spec(channels), pair_spec, pair_spec] + far_specs,
        scratch(near),
        cost(1, 12),
        "middle",
    )
    halos = exchange(sent)

    facing_labels = facing_tile(own_labels)
    squeezed_2, facing_labels = lax.optimization_barrier((squeezed_2, facing_labels))
    facing_labels = facing_labels.T
    centre = squeezed_2
    by_row_spec = "rows", pl.BlockSpec((BLOCK, columns, 2 * bins), lambda step: (step, 0, 0))
    stream_2, activated_2, by_row, by_column = call(
        functools.partial(head_kernel, far, steps),
        (centre, *halos, stream_1, ones, convs[1], ups[1], gains[2], head, bias),
        [whole(centre)] + [whole(halo) for halo in halos] + [bf_spec]
        + [whole(array) for array in (ones, convs[1], ups[1], gains[2], head, bias)],
        [
            halves(F32, channels),
            pair_shape,
            jax.ShapeDtypeStruct((half, columns, 2 * bins), BF16),
            jax.ShapeDtypeStruct((2, half, columns // 2, 2 * bins), BF16),
        ],
        [
            strip_spec(channels),
            pair_spec,
            by_row_spec,
            ("halves", pl.BlockSpec((2, BLOCK, columns // 2, 2 * bins), lambda step: (0, step, 0, 0))),
        ],
        scratch(far),
        cost(1, 14),
        "head",
    )
    facing = facing_logits(by_column.reshape(rows, columns // 2, 2 * bins))

    numbers = jnp.arange(bins, dtype=jnp.int32)

    def onehot(values):
        return (values[:, :, None] == numbers).astype(F32)

    targets = jnp.concatenate(
        [
            0.5 * (onehot(own_labels[part]) + onehot(facing_labels[part]))
            for part in (slice(0, half), slice(half, rows))
        ],
        axis=2,
    ).astype(BF16)

    inner = BLOCK // ROWS
    mirrored_logits = [array for piece in facing for array in piece]
    grad_2, conv_grad_2, *sent = call(
        functools.partial(loss_kernel, far, steps, inner, tuple(len(piece) for piece in facing)),
        (by_row, *mirrored_logits, targets, stream_2, activated_2, ones, head_back, group, ups_back[1]),
        [
            by_row_spec,
            *(("whole", pl.BlockSpec((array.shape[0], BLOCK, 2 * bins), lambda step: (0, step, 0)))
              for array in mirrored_logits),
            by_row_spec,
            bf_spec,
            pair_spec,
        ]
        + [whole(array) for array in (ones, head_back, group, ups_back[1])],
        [halves(F32, channels), pair_shape] + far_shapes,
        [strip_spec(channels), pair_spec] + far_specs,
        [pltpu.VMEM((BLOCK, columns, 2 * bins), F32)],
        cost(0, 18),
        "loss",
    )
    halos = exchange(sent)

    centre = conv_grad_2
    grad_1, conv_grad_1, *sent = call(
        functools.partial(back_kernel, far, near, steps),
        (centre, *halos, convs_back[1], squeezed_2, downs_back[1], stream_1, ones, gains[1], grad_2, activated_1, ups_back[0]),
        [whole(centre)] + [whole(halo) for halo in halos]
        + [
            whole(convs_back[1]),
            pair_spec,
            whole(downs_back[1]),
            bf_spec,
            whole(ones),
            whole(gains[1]),
            bf_spec,
            pair_spec,
            whole(ups_back[0]),
        ],
        [halves(F32, channels), pair_shape] + near_shapes,
        [strip_spec(channels), pair_spec] + near_specs,
        scratch(far),
        cost(1, 20),
        "back",
    )
    halos = exchange(sent)

    centre = conv_grad_1
    (grad_0,) = call(
        functools.partial(final_kernel, near),
        (centre, *halos, convs_back[0], squeezed_1, downs_back[0], split, centring, ones, gains[0], grad_1),
        [whole(centre)] + [whole(halo) for halo in halos]
        + [
            whole(convs_back[0]),
            pair_spec,
            whole(downs_back[0]),
            bf_spec,
            whole(centring),
            whole(ones),
            whole(gains[0]),
            bf_spec,
        ],
        [halves(F32, channels)],
        [strip_spec(channels)],
        scratch(near),
        cost(1, 16),
        "final",
    )
    return grad_0.reshape(features.shape)


def solution(mesh):
    return jax.shard_map(
        shards,
        mesh=mesh,
        in_specs=(
            P(("dp", "row"), "col", None),
            P(("dp", "row", "col"), None),
            P(),
            P(),
            P(),
            P(),
            P(),
            P(),
        ),
        out_specs=P(("dp", "row"), "col", None),
        check_vma=False,
    )
```

```python
import functools
import math

import jax
import jax.numpy as jnp
from jax import lax
from jax.experimental import pallas as pl
from jax.experimental.pallas import tpu as pltpu
from jax.sharding import PartitionSpec as P

epsilon = 1e-05
F32 = jnp.float32
BF16 = jnp.bfloat16
BLOCK = 16
ROWS = 16
EDGE = 8
PAD = 16


def lane_low(shape):
    return lax.broadcasted_iota(jnp.int32, shape, len(shape) - 1) < shape[-1] // 2


def lane_sums(values, ones):
    return jnp.sum(values, -1, keepdims=True)


def standardize(centred, ones):
    inverse = lax.rsqrt(lane_sums(centred * centred, ones) + epsilon * centred.shape[-1])
    return centred * inverse, inverse


def elu(values):
    return jnp.maximum(values, jnp.exp(jnp.minimum(values, 0.0)) - 1.0)


def slope_from_elu(activated):
    return 1.0 + jnp.minimum(activated, 0.0)


def standardize_back(standard, inverse, upstream, ones):
    return inverse * (upstream - standard * lane_sums(upstream * standard, ones))


def side_by_side(values):
    count = values.shape[0] // 2
    return jnp.concatenate([values[:count], values[count:]], axis=1)


def stacked(values):
    width = values.shape[1] // 2
    return jnp.concatenate([values[:, :width], values[:, width:]], axis=0)


def swapped(values):
    flat = values.reshape(-1, values.shape[-1])
    return pltpu.roll(flat, flat.shape[1] // 2, 1).reshape(values.shape)


def squeeze(centred, ones, gain, down):
    standard, unused = standardize(centred, ones)
    entered = elu(standard * gain).astype(BF16)
    return elu(jnp.dot(side_by_side(entered), down, preferred_element_type=F32))


def widened(activated, weight):
    return stacked(jnp.dot(jnp.concatenate([activated, activated], axis=1), weight, preferred_element_type=F32))


def store_edges(values, refs, spacing, step, steps):
    top, bottom, left, right = refs
    middle = values.shape[1] // 2
    left[...] = values[:, :EDGE].astype(BF16)
    right[...] = values[:, values.shape[1] - EDGE :].astype(BF16)
    count = min(ROWS, spacing)
    low = lane_low((count, middle, values.shape[2]))
    taken = spacing // count

    @pl.when((step < taken) & (top is not None))
    def _():
        if top is None:
            return
        sent = values[:count]
        rows = pl.ds(jnp.minimum(step, taken - 1) * count, count)
        top[rows] = jnp.where(low, sent[:, :middle], swapped(sent[:, middle:])).astype(BF16)

    @pl.when((step >= steps - taken) & (bottom is not None))
    def _():
        if bottom is None:
            return
        sent = values[ROWS - count :]
        rows = pl.ds(jnp.maximum(step - (steps - taken), 0) * count, count)
        bottom[rows] = jnp.where(low, swapped(sent[:, :middle]), sent[:, middle:]).astype(BF16)


def fill_padded(padded, centre, halos, spacing):
    above, below, before, after = halos
    half, columns, lanes = centre.shape
    middle = columns // 2

    def lay(row, carry):
        padded[spacing + row, PAD : PAD + columns] = centre[row]
        padded[spacing + row, PAD - EDGE : PAD] = before[row]
        padded[spacing + row, PAD + columns : PAD + columns + EDGE] = after[row]
        return carry

    lax.fori_loop(0, half, lay, 0)
    wide, slim = lane_low((middle, lanes)), lane_low((EDGE, lanes))

    def put(row, start, low, first, second):
        padded[row, start : start + low.shape[0]] = jnp.where(low, first, second).astype(BF16)

    def read(array, row):
        return array[row].astype(F32)

    for row in range(spacing):
        own = swapped(read(centre, half - spacing + row))
        sent = read(above, row)
        put(row, PAD, wide, sent, own[:middle])
        put(row, PAD + middle, wide, swapped(sent), own[middle:])
        edge = half - spacing + row
        put(row, PAD - EDGE, slim, swapped(read(before, half + row)), swapped(read(before, edge)))
        put(row, PAD + columns, slim, read(after, half + row), swapped(read(after, edge)))
        place = spacing + half + row
        own = swapped(read(centre, row))
        sent = read(below, row)
        put(place, PAD, wide, own[:middle], swapped(sent))
        put(place, PAD + middle, wide, own[middle:], sent)
        corner = half + spacing + row
        put(place, PAD - EDGE, slim, swapped(read(before, row)), read(before, corner))
        put(place, PAD + columns, slim, swapped(read(after, row)), swapped(read(after, corner)))


def convolve(padded, kernel, taps, spacing, step, columns):
    width = columns + 2 * PAD
    lanes = padded.shape[2]
    parts = [padded[pl.ds(step * ROWS + tap * spacing, ROWS)] for tap in range(3)]
    joined = jnp.concatenate(parts, axis=2).reshape(ROWS * width, 3 * lanes)
    taps[...] = jnp.dot(joined, kernel[...], preferred_element_type=F32).reshape(ROWS, width, 3 * lanes)
    total = taps[:, PAD : PAD + columns, lanes : 2 * lanes]
    if spacing % EDGE:
        outer = taps[:, PAD - EDGE : PAD + columns, :lanes]
        start = PAD - EDGE + 2 * spacing
        outer = outer + taps[:, start : start + columns + EDGE, 2 * lanes :]
        total = total + outer[:, EDGE - spacing : EDGE - spacing + columns]
    else:
        total = total + taps[:, PAD - spacing : PAD - spacing + columns, :lanes]
        total = total + taps[:, PAD + spacing : PAD + spacing + columns, 2 * lanes :]
    return total.reshape(ROWS * columns, lanes)


def strip(reference):
    return reference[...].reshape(-1, reference.shape[-1])


def over_strips(body, kinds, first, *refs):
    inner = BLOCK // ROWS

    def one(place, carry):
        rows = pl.ds(place * ROWS, ROWS)
        views = []
        for kind, ref in zip(kinds, refs):
            views.append(ref.at[:, rows] if kind == "halves" else ref.at[rows] if kind == "rows" else ref)
        body((pl.program_id(0) + first) * inner + place, *views)
        return carry

    lax.fori_loop(0, inner, one, 0)


def entry_kernel(spacing, steps, step, features, centring, ones, gain, down, squeezed, *edges):
    centred = jnp.dot(strip(features), centring[...], preferred_element_type=F32)
    values = squeeze(centred, ones, gain[...], down[...]).reshape(squeezed.shape)
    squeezed[...] = values.astype(BF16)
    store_edges(values, edges, spacing, step, steps)


def middle_kernel(near, far, steps, step, centre, *rest):
    halos, rest = rest[:4], rest[4:]
    features, centring, ones, kernel, up, gain, down, stream_out, activated_out, squeezed, *rest = rest
    edges, (padded, taps) = rest[:4], rest[4:]
    columns = centre.shape[1]

    @pl.when(step == 0)
    def _():
        fill_padded(padded, centre, halos, near)

    activated = elu(convolve(padded, kernel, taps, near, step, columns)).astype(BF16)
    activated_out[...] = activated.reshape(activated_out.shape)
    stream = jnp.dot(strip(features), centring[...], preferred_element_type=F32) + widened(activated, up[...])
    stream_out[...] = stream.reshape(stream_out.shape)
    values = squeeze(stream, ones, gain[...], down[...]).reshape(squeezed.shape)
    squeezed[...] = values.astype(BF16)
    store_edges(values, edges, far, step, steps)


def head_kernel(near, steps, step, centre, *rest):
    halos, rest = rest[:4], rest[4:]
    stream_in, ones, kernel, up, gain, head, bias, stream_out, activated_out, by_row, *by_column, padded, taps = rest
    columns = centre.shape[1]

    @pl.when(step == 0)
    def _():
        fill_padded(padded, centre, halos, near)

    activated = elu(convolve(padded, kernel, taps, near, step, columns)).astype(BF16)
    activated_out[...] = activated.reshape(activated_out.shape)
    stream = strip(stream_in) + widened(activated, up[...])
    stream_out[...] = stream.reshape(stream_out.shape)
    standard, unused = standardize(stream, ones)
    entered = (standard * gain[...]).astype(BF16).reshape(2, ROWS, columns, stream.shape[1])
    pairs = jnp.concatenate([entered[0], entered[1]], axis=2).reshape(ROWS * columns, -1)
    logits = jnp.dot(pairs, head[...], preferred_element_type=F32) + bias[...]
    by_row[...] = logits.astype(BF16).reshape(by_row.shape)
    pairs = jnp.concatenate([entered[:, :, : columns // 2], entered[:, :, columns // 2 :]], axis=3)
    logits = jnp.dot(pairs.reshape(ROWS * columns, -1), head[...], preferred_element_type=F32) + bias[...]
    logits = logits.astype(BF16).reshape(2, ROWS, columns // 2, -1)
    place = 0
    for piece in by_column:
        piece[...] = logits[:, :, place : place + piece.shape[2]]
        place += piece.shape[2]


def loss_kernel(spacing, steps, inner, count, ends, step, by_row, *rest):
    facing, rest = rest[:count], rest[count:]
    targets, stream, activated, ones, head, group, up, *rest = rest
    *outputs, turned = rest
    grad_out, conv_out, left, right, *far = outputs[-4 - sum(ends) :]
    top = far[0] if ends[0] else None
    bottom = far[-1] if ends[1] else None
    edges = top, bottom, left, right

    @pl.when(step % inner == 0)
    def _():
        turned[...] = jnp.swapaxes(sum(array[...].astype(F32) for array in facing), 0, 1)

    start = (step % inner) * ROWS
    columns, lanes = by_row.shape[1:]
    symmetric = 0.5 * (by_row[...].astype(F32) + turned[pl.ds(start, ROWS)])
    exponent = jnp.exp(symmetric).reshape(ROWS * columns, lanes)
    upper = exponent.astype(BF16)
    lower = (exponent - upper.astype(F32)).astype(BF16)
    total = jnp.dot(upper, group[...], preferred_element_type=F32) + jnp.dot(
        lower, group[...], preferred_element_type=F32
    )
    logit_grad = (exponent / total - targets[...].astype(F32).reshape(exponent.shape)).astype(BF16)
    back = widened(logit_grad, head[...])
    standard, inverse = standardize(strip(stream), ones)
    grad = standardize_back(standard, inverse, back, ones)
    grad_out[...] = grad.reshape(grad_out.shape)
    values = jnp.dot(side_by_side(grad.astype(BF16)), up[...], preferred_element_type=F32)
    values = values * slope_from_elu(strip(activated).astype(F32))
    values = values.reshape(conv_out.shape)
    conv_out[...] = values.astype(BF16)
    store_edges(values, edges, spacing, step, steps)


def back_strip(spacing, step, centre, padded, taps, kernel, squeezed, down, centred, ones, gain, upstream):
    columns = centre.shape[1]
    lowered = convolve(padded, kernel, taps, spacing, step, columns)
    lowered = lowered * slope_from_elu(strip(squeezed).astype(F32))
    entered = stacked(jnp.dot(lowered.astype(BF16), down[...], preferred_element_type=F32))
    standard, inverse = standardize(centred, ones)
    scale = gain[...]
    entered = entered * (jnp.exp2(jnp.minimum(standard * (scale * math.log2(math.e)), 0.0)) * scale)
    entered = entered - jnp.sum(entered, -1, keepdims=True) * (1.0 / entered.shape[-1])
    return strip(upstream) + standardize_back(standard, inverse, entered, ones)


def back_kernel(near, far, steps, step, centre, *rest):
    halos, rest = rest[:4], rest[4:]
    kernel, squeezed, down, stream, ones, gain, upstream, activated, up, grad_out, conv_out, *rest = rest
    edges, (padded, taps) = rest[:4], rest[4:]

    @pl.when(step == 0)
    def _():
        fill_padded(padded, centre, halos, near)

    grad = back_strip(near, step, centre, padded, taps, kernel, squeezed, down, strip(stream), ones, gain, upstream)
    grad_out[...] = grad.reshape(grad_out.shape)
    values = jnp.dot(side_by_side(grad.astype(BF16)), up[...], preferred_element_type=F32)
    values = values * slope_from_elu(strip(activated).astype(F32))
    values = values.reshape(conv_out.shape)
    conv_out[...] = values.astype(BF16)
    store_edges(values, edges, far, step, steps)


def final_kernel(near, step, centre, *rest):
    halos, rest = rest[:4], rest[4:]
    kernel, squeezed, down, features, centring, ones, gain, upstream, grad_out, padded, taps = rest

    @pl.when(step == 0)
    def _():
        fill_padded(padded, centre, halos, near)

    centred = jnp.dot(strip(features), centring[...], preferred_element_type=F32)
    grad = back_strip(near, step, centre, padded, taps, kernel, squeezed, down, centred, ones, gain, upstream)
    grad_out[...] = grad.reshape(grad_out.shape)


def shifted(values, axis, move):
    count = lax.axis_size(axis)
    return lax.ppermute(values, axis, [(i, i + move) for i in range(count) if 0 <= i + move < count])


def exchange(edges):
    top, bottom, left, right = edges
    above = shifted(bottom, "row", 1)
    below = shifted(top, "row", -1)
    before = jnp.concatenate([right, above[:, -EDGE:], below[:, -EDGE:]], axis=0)
    after = jnp.concatenate([left, above[:, :EDGE], below[:, :EDGE]], axis=0)
    return above, below, shifted(before, "col", 1), shifted(after, "col", -1)


def facing_tile(tile):
    rows, cols = lax.axis_size("row"), lax.axis_size("col")
    if rows == cols:
        pairs = [(row * cols + col, col * cols + row) for row in range(rows) for col in range(cols)]
        return lax.ppermute(tile, ("row", "col"), pairs)
    if cols % rows:
        raise ValueError("unsupported mesh")
    times = cols // rows
    height = tile.shape[0] // times
    place = lax.axis_index("col") % times
    received = []
    for turn in range(times):
        piece = lax.dynamic_slice_in_dim(tile, ((place + turn) % times) * height, height, axis=0)
        pairs = [
            (row * cols + col, (col // times) * cols + times * row + (col % times + turn) % times)
            for row in range(rows)
            for col in range(cols)
        ]
        received.append(lax.ppermute(piece, ("row", "col"), pairs))
    stacked = jnp.stack(received)
    pieces = [
        lax.dynamic_index_in_dim(stacked, (place - source) % times, axis=0, keepdims=False)
        for source in range(times)
    ]
    return jnp.concatenate(pieces, axis=1)


def facing_logits(by_column):
    rows, cols = lax.axis_size("row"), lax.axis_size("col")
    if rows == cols and rows % 2 == 0:
        straight, *around = by_column
        places = [(row, col) for row in range(rows) for col in range(cols)]
        part = rows // 2
        far = [(row, col) for row, col in places if row // part != col // part]
        close = [(row, col) for row, col in places if row // part == col // part]
        number = lambda row, col: row * cols + col
        other = lambda row: (row + part) % rows
        move = lambda array, pairs: lax.ppermute(array, ("row", "col"), pairs)
        hops = [move(array, [(number(row, col), number(other(row), col)) for row, col in far]) for array in around]
        straight = move(straight, [(number(row, col), number(col, row)) for row, col in places])
        near = [move(array, [(number(row, col), number(col, row)) for row, col in close]) for array in around]
        hops = [move(array, [(number(other(row), col), number(col, row)) for row, col in far]) for array in hops]
        return [[straight]] + [list(pair) for pair in zip(hops, near)]
    tile = jnp.concatenate(by_column, axis=1)
    if rows == cols:
        tile = facing_tile(tile)
    else:
        bins = tile.shape[2] // 2
        tile = facing_tile(jnp.concatenate([tile[..., :bins], tile[..., bins:]], axis=1))
        half = tile.shape[1] // 2
        tile = jnp.concatenate([tile[:, :half], tile[:, half:]], axis=2)
    return [[tile]]


def diagonal(weight):
    zeros = jnp.zeros_like(weight)
    return jnp.concatenate(
        [jnp.concatenate([weight, zeros], axis=1), jnp.concatenate([zeros, weight], axis=1)], axis=0
    )


def dilated_weights(blocks):
    return jnp.concatenate(
        [jnp.concatenate([diagonal(block) for block in line], axis=1) for line in blocks], axis=0
    )


def two_parts(weight):
    centred = weight - jnp.mean(weight, axis=1, keepdims=True)
    upper = centred.astype(BF16).astype(F32)
    return jnp.concatenate([diagonal(upper), diagonal(centred - upper)], axis=0)


def derived(norm_gain, w_down, w_conv, w_up, w_head, head_bias):
    channels, bins = w_head.shape
    gains = [norm_gain[index : index + 1] * math.sqrt(channels) for index in range(3)]
    down = [w_down[index].astype(F32) for index in range(2)]
    up = [w_up[index].astype(F32) for index in range(2)]
    conv = [[[w_conv[index, row, col].astype(F32) for col in range(3)] for row in range(3)] for index in range(2)]
    back = [[[conv[index][2 - row][2 - col].T for col in range(3)] for row in range(3)] for index in range(2)]
    head = w_head[...].astype(F32)
    first = lax.broadcasted_iota(jnp.int32, (channels, channels), 0)
    second = lax.broadcasted_iota(jnp.int32, (channels, channels), 1)
    matrices = dict(
        downs=[diagonal(weight) for weight in down],
        downs_back=[diagonal(weight.T) for weight in down],
        ups=[two_parts(weight) for weight in up],
        ups_back=[diagonal(weight.T) for weight in up],
        convs=[dilated_weights(blocks) for blocks in conv],
        convs_back=[dilated_weights(blocks) for blocks in back],
        head=diagonal(head),
        head_back=two_parts(head.T * gains[2]),
        group=diagonal(jnp.ones((bins, bins), F32)),
        centring=jnp.where(first == second, 1.0, 0.0) - 1.0 / channels,
        ones=jnp.ones((channels, channels), F32),
    )
    matrices = jax.tree.map(lambda array: array.astype(BF16), matrices)
    bias = head_bias[...]
    return dict(matrices, gains=gains, bias=jnp.concatenate([bias, bias], axis=1))


def derive(*sources):
    shapes = jax.eval_shape(derived, *sources)
    leaves, tree = jax.tree.flatten(shapes)

    def kernel(*refs):
        results = jax.tree.leaves(derived(*refs[: len(sources)]))
        for ref, result in zip(refs[len(sources) :], results):
            ref[...] = result

    made = pl.pallas_call(
        kernel,
        grid=(1,),
        in_specs=[pl.BlockSpec(array.shape, lambda step, rank=array.ndim: (0,) * rank) for array in sources],
        out_specs=[pl.BlockSpec(leaf.shape, lambda step: (0, 0)) for leaf in leaves],
        out_shape=leaves,
        compiler_params=pltpu.CompilerParams(vmem_limit_bytes=60 * 1024 * 1024),
        name="weights",
    )(*sources)
    return jax.tree.unflatten(tree, made)


def shards(features, labels, norm_gain, w_down, w_conv, w_up, w_head, head_bias):
    rows, columns, channels = features.shape
    narrow = w_down.shape[2]
    bins = w_head.shape[1]
    half = rows // 2
    steps = half // ROWS
    lanes = 2 * narrow
    near, far = 4, 8

    made = derive(norm_gain, w_down, w_conv, w_up, w_head, head_bias[None])
    gains, bias, centring, ones, group = (made[name] for name in ("gains", "bias", "centring", "ones", "group"))
    downs, downs_back, ups, ups_back = (made[name] for name in ("downs", "downs_back", "ups", "ups_back"))
    convs, convs_back, head, head_back = (made[name] for name in ("convs", "convs_back", "head", "head_back"))

    def whole(array):
        zeros = (0,) * len(array.shape)
        return "whole", pl.BlockSpec(array.shape, lambda step: zeros)

    def strip_spec(width):
        return "halves", pl.BlockSpec((2, BLOCK, columns, width), lambda step: (0, step, 0, 0))

    def halves(dtype, width):
        return jax.ShapeDtypeStruct((2, half, columns, width), dtype)

    pair_spec = "rows", pl.BlockSpec((BLOCK, columns, lanes), lambda step: (step, 0, 0))
    pair_shape = jax.ShapeDtypeStruct((half, columns, lanes), BF16)

    def edges(spacing):
        shapes = [jax.ShapeDtypeStruct((spacing, columns // 2, lanes), BF16)] * 2
        shapes += [jax.ShapeDtypeStruct((half, EDGE, lanes), BF16)] * 2
        sides = "rows", pl.BlockSpec((BLOCK, EDGE, lanes), lambda step: (step, 0, 0))
        return shapes, [whole(shapes[0]), whole(shapes[1]), sides, sides]

    def scratch(spacing):
        width = columns + 2 * PAD
        return [
            pltpu.VMEM((half + 2 * spacing, width, lanes), BF16),
            pltpu.VMEM((ROWS, width, 3 * lanes), F32),
        ]

    def cost(convolutions, passes):
        pixels = rows * columns
        return pl.CostEstimate(
            flops=pixels * (convolutions * 18 * narrow * narrow + 4 * narrow * channels),
            bytes_accessed=pixels * channels * passes,
            transcendentals=pixels * channels,
        )

    def call(body, inputs, specs, shapes, out_specs, scratch_shapes, estimate, name):
        kinds = [kind for kind, spec in specs + out_specs] + ["whole"] * len(scratch_shapes)
        return pl.pallas_call(
            functools.partial(over_strips, body, kinds, 0),
            grid=(half // BLOCK,),
            in_specs=[spec for kind, spec in specs],
            out_specs=[spec for kind, spec in out_specs],
            out_shape=shapes,
            scratch_shapes=scratch_shapes,
            compiler_params=pltpu.CompilerParams(vmem_limit_bytes=56 * 1024 * 1024),
            cost_estimate=estimate,
            name=name,
        )(*inputs)

    own_labels = lax.all_to_all(labels, "col", split_axis=1, concat_axis=0, tiled=True)
    facing_labels = facing_tile(own_labels)
    features, own_labels, facing_labels = lax.optimization_barrier((features, own_labels, facing_labels))
    facing_labels = facing_labels.T
    split = features.reshape(2, half, columns, channels)
    bf_spec = strip_spec(channels)
    near_shapes, near_specs = edges(near)
    far_shapes, far_specs = edges(far)

    squeezed_1, *sent = call(
        functools.partial(entry_kernel, near, steps),
        (split, centring, ones, gains[0], downs[0]),
        [bf_spec] + [whole(array) for array in (centring, ones, gains[0], downs[0])],
        [pair_shape] + near_shapes,
        [pair_spec] + near_specs,
        [],
        cost(0, 4),
        "entry",
    )
    halos = exchange(sent)

    centre = squeezed_1
    stream_1, activated_1, squeezed_2, *sent = call(
        functools.partial(middle_kernel, near, far, steps),
        (centre, *halos, split, centring, ones, convs[0], ups[0], gains[1], downs[1]),
        [whole(centre)] + [whole(halo) for halo in halos] + [bf_spec]
        + [whole(array) for array in (centring, ones, convs[0], ups[0], gains[1], downs[1])],
        [halves(F32, channels), pair_shape, pair_shape] + far_shapes,
        [strip_spec(channels), pair_spec, pair_spec] + far_specs,
        scratch(near),
        cost(1, 12),
        "middle",
    )
    halos = exchange(sent)

    centre = squeezed_2
    by_row_spec = "rows", pl.BlockSpec((BLOCK, columns, 2 * bins), lambda step: (step, 0, 0))
    parts = [columns // 4, columns // 8, columns // 8]
    stream_2, activated_2, by_row, *by_column = call(
        functools.partial(head_kernel, far, steps),
        (centre, *halos, stream_1, ones, convs[1], ups[1], gains[2], head, bias),
        [whole(centre)] + [whole(halo) for halo in halos] + [bf_spec]
        + [whole(array) for array in (ones, convs[1], ups[1], gains[2], head, bias)],
        [
            halves(F32, channels),
            pair_shape,
            jax.ShapeDtypeStruct((half, columns, 2 * bins), BF16),
            *(jax.ShapeDtypeStruct((2, half, part, 2 * bins), BF16) for part in parts),
        ],
        [
            strip_spec(channels),
            pair_spec,
            by_row_spec,
            *(("halves", pl.BlockSpec((2, BLOCK, part, 2 * bins), lambda step: (0, step, 0, 0))) for part in parts),
        ],
        scratch(far),
        cost(1, 14),
        "head",
    )
    facing = facing_logits([piece.reshape(rows, piece.shape[2], 2 * bins) for piece in by_column])

    numbers = jnp.arange(bins, dtype=jnp.int32)

    def onehot(values):
        return (values[:, :, None] == numbers).astype(F32)

    targets = jnp.concatenate(
        [
            0.5 * (onehot(own_labels[part]) + onehot(facing_labels[part]))
            for part in (slice(0, half), slice(half, rows))
        ],
        axis=2,
    ).astype(BF16)

    taken = 0
    outputs = []
    sent = [None, None, None, None]
    for index, piece in enumerate(facing):
        blocks = piece[0].shape[1] // BLOCK
        ends = taken == 0, index == len(facing) - 1

        def moved(spec, first=taken):
            kind, block = spec
            return kind, pl.BlockSpec(
                block.block_shape,
                lambda step: tuple(
                    place + first * (rank == (1 if kind == "halves" else 0))
                    for rank, place in enumerate(block.index_map(step))
                ),
            )

        weights = [ones, head_back, group, ups_back[1]]
        side_shape, side_spec = far_shapes[2], moved(far_specs[2])
        specs = [moved(by_row_spec)]
        specs += [("whole", pl.BlockSpec((columns, BLOCK, 2 * bins), lambda step: (0, step, 0)))] * len(piece)
        specs += [moved(by_row_spec), moved(bf_spec), moved(pair_spec)] + [whole(array) for array in weights]
        inputs = [by_row, *piece, targets, stream_2, activated_2, *weights]
        out_shapes = [halves(F32, channels), pair_shape, side_shape, side_shape]
        out_specs = [moved(bf_spec), moved(pair_spec), side_spec, side_spec]
        for place in range(2):
            if ends[place]:
                out_shapes.append(far_shapes[place])
                out_specs.append(far_specs[place])
        kinds = [kind for kind, spec in specs] + ["whole"] * len(outputs)
        kinds += [kind for kind, spec in out_specs] + ["whole"]
        body = functools.partial(loss_kernel, far, steps, BLOCK // ROWS, len(piece), ends)
        results = pl.pallas_call(
            functools.partial(over_strips, body, kinds, taken),
            grid=(blocks,),
            in_specs=[spec for kind, spec in specs] + [pl.BlockSpec(memory_space=pl.ANY)] * len(outputs),
            out_specs=[spec for kind, spec in out_specs],
            out_shape=out_shapes,
            input_output_aliases={len(inputs) + place: place for place in range(len(outputs))},
            scratch_shapes=[pltpu.VMEM((BLOCK, columns, 2 * bins), F32)],
            compiler_params=pltpu.CompilerParams(vmem_limit_bytes=56 * 1024 * 1024),
            cost_estimate=cost(0, 18),
            name="loss",
        )(*inputs, *outputs)
        outputs = list(results[:4])
        if ends[0]:
            sent[0] = results[4]
        if ends[1]:
            sent[1] = results[-1]
        taken += blocks
    grad_2, conv_grad_2, *sent[2:] = outputs
    halos = exchange(sent)

    centre = conv_grad_2
    grad_1, conv_grad_1, *sent = call(
        functools.partial(back_kernel, far, near, steps),
        (centre, *halos, convs_back[1], squeezed_2, downs_back[1], stream_1, ones, gains[1], grad_2, activated_1, ups_back[0]),
        [whole(centre)] + [whole(halo) for halo in halos]
        + [
            whole(convs_back[1]),
            pair_spec,
            whole(downs_back[1]),
            bf_spec,
            whole(ones),
            whole(gains[1]),
            bf_spec,
            pair_spec,
            whole(ups_back[0]),
        ],
        [halves(F32, channels), pair_shape] + near_shapes,
        [strip_spec(channels), pair_spec] + near_specs,
        scratch(far),
        cost(1, 20),
        "back",
    )
    halos = exchange(sent)

    centre = conv_grad_1
    (grad_0,) = call(
        functools.partial(final_kernel, near),
        (centre, *halos, convs_back[0], squeezed_1, downs_back[0], split, centring, ones, gains[0], grad_1),
        [whole(centre)] + [whole(halo) for halo in halos]
        + [
            whole(convs_back[0]),
            pair_spec,
            whole(downs_back[0]),
            bf_spec,
            whole(centring),
            whole(ones),
            whole(gains[0]),
            bf_spec,
        ],
        [halves(F32, channels)],
        [strip_spec(channels)],
        scratch(near),
        cost(1, 16),
        "final",
    )
    return grad_0.reshape(features.shape)


def solution(mesh):
    return jax.shard_map(
        shards,
        mesh=mesh,
        in_specs=(
            P(("dp", "row"), "col", None),
            P(("dp", "row", "col"), None),
            P(),
            P(),
            P(),
            P(),
            P(),
            P(),
        ),
        out_specs=P(("dp", "row"), "col", None),
        check_vma=False,
    )
```

```python
import functools
import math

import jax
import jax.numpy as jnp
from jax import lax
from jax.experimental import pallas as pl
from jax.experimental.pallas import tpu as pltpu
from jax.sharding import PartitionSpec as P

epsilon = 1e-05
F32 = jnp.float32
BF16 = jnp.bfloat16
BLOCK = 16
ROWS = 16
EDGE = 8
PAD = 16


def lane_low(shape):
    return lax.broadcasted_iota(jnp.int32, shape, len(shape) - 1) < shape[-1] // 2


def lane_sums(values, ones):
    return jnp.sum(values, -1, keepdims=True)


def standardize(centred, ones):
    inverse = lax.rsqrt(lane_sums(centred * centred, ones) + epsilon * centred.shape[-1])
    return centred * inverse, inverse


def elu(values):
    return jnp.maximum(values, jnp.exp(jnp.minimum(values, 0.0)) - 1.0)


def slope_from_elu(activated):
    return 1.0 + jnp.minimum(activated, 0.0)


def standardize_back(standard, inverse, upstream, ones):
    return inverse * (upstream - standard * lane_sums(upstream * standard, ones))


def side_by_side(values):
    count = values.shape[0] // 2
    return jnp.concatenate([values[:count], values[count:]], axis=1)


def stacked(values):
    width = values.shape[1] // 2
    return jnp.concatenate([values[:, :width], values[:, width:]], axis=0)


def swapped(values):
    flat = values.reshape(-1, values.shape[-1])
    return pltpu.roll(flat, flat.shape[1] // 2, 1).reshape(values.shape)


def squeeze(centred, ones, gain, down):
    standard, unused = standardize(centred, ones)
    entered = elu(standard * gain).astype(BF16)
    return elu(jnp.dot(side_by_side(entered), down, preferred_element_type=F32))


def widened(activated, weight):
    return stacked(jnp.dot(jnp.concatenate([activated, activated], axis=1), weight, preferred_element_type=F32))


def store_edges(values, refs, spacing, step, steps):
    top, bottom, left, right = refs
    middle = values.shape[1] // 2
    left[...] = values[:, :EDGE].astype(BF16)
    right[...] = values[:, values.shape[1] - EDGE :].astype(BF16)
    count = min(ROWS, spacing)
    low = lane_low((count, middle, values.shape[2]))
    taken = spacing // count

    @pl.when((step < taken) & (top is not None))
    def _():
        if top is None:
            return
        sent = values[:count]
        rows = pl.ds(jnp.minimum(step, taken - 1) * count, count)
        top[rows] = jnp.where(low, sent[:, :middle], swapped(sent[:, middle:])).astype(BF16)

    @pl.when((step >= steps - taken) & (bottom is not None))
    def _():
        if bottom is None:
            return
        sent = values[ROWS - count :]
        rows = pl.ds(jnp.maximum(step - (steps - taken), 0) * count, count)
        bottom[rows] = jnp.where(low, swapped(sent[:, :middle]), sent[:, middle:]).astype(BF16)


def fill_padded(padded, centre, halos, spacing):
    above, below, before, after = halos
    half, columns, lanes = centre.shape
    middle = columns // 2

    def lay(row, carry):
        padded[spacing + row, PAD : PAD + columns] = centre[row]
        padded[spacing + row, PAD - EDGE : PAD] = before[row]
        padded[spacing + row, PAD + columns : PAD + columns + EDGE] = after[row]
        return carry

    lax.fori_loop(0, half, lay, 0)
    wide, slim = lane_low((middle, lanes)), lane_low((EDGE, lanes))

    def put(row, start, low, first, second):
        padded[row, start : start + low.shape[0]] = jnp.where(low, first, second).astype(BF16)

    def read(array, row):
        return array[row].astype(F32)

    for row in range(spacing):
        own = swapped(read(centre, half - spacing + row))
        sent = read(above, row)
        put(row, PAD, wide, sent, own[:middle])
        put(row, PAD + middle, wide, swapped(sent), own[middle:])
        edge = half - spacing + row
        put(row, PAD - EDGE, slim, swapped(read(before, half + row)), swapped(read(before, edge)))
        put(row, PAD + columns, slim, read(after, half + row), swapped(read(after, edge)))
        place = spacing + half + row
        own = swapped(read(centre, row))
        sent = read(below, row)
        put(place, PAD, wide, own[:middle], swapped(sent))
        put(place, PAD + middle, wide, own[middle:], sent)
        corner = half + spacing + row
        put(place, PAD - EDGE, slim, swapped(read(before, row)), read(before, corner))
        put(place, PAD + columns, slim, swapped(read(after, row)), swapped(read(after, corner)))


def convolve(padded, kernel, taps, spacing, step, columns):
    width = columns + 2 * PAD
    lanes = padded.shape[2]
    parts = [padded[pl.ds(step * ROWS + tap * spacing, ROWS)] for tap in range(3)]
    joined = jnp.concatenate(parts, axis=2).reshape(ROWS * width, 3 * lanes)
    taps[...] = jnp.dot(joined, kernel[...], preferred_element_type=F32).reshape(ROWS, width, 3 * lanes)
    total = taps[:, PAD : PAD + columns, lanes : 2 * lanes]
    if spacing % EDGE:
        outer = taps[:, PAD - EDGE : PAD + columns, :lanes]
        start = PAD - EDGE + 2 * spacing
        outer = outer + taps[:, start : start + columns + EDGE, 2 * lanes :]
        total = total + outer[:, EDGE - spacing : EDGE - spacing + columns]
    else:
        total = total + taps[:, PAD - spacing : PAD - spacing + columns, :lanes]
        total = total + taps[:, PAD + spacing : PAD + spacing + columns, 2 * lanes :]
    return total.reshape(ROWS * columns, lanes)


def strip(reference):
    return reference[...].reshape(-1, reference.shape[-1])


def over_strips(body, kinds, first, *refs):
    inner = BLOCK // ROWS

    def one(place, carry):
        rows = pl.ds(place * ROWS, ROWS)
        views = []
        for kind, ref in zip(kinds, refs):
            views.append(ref.at[:, rows] if kind == "halves" else ref.at[rows] if kind == "rows" else ref)
        body((pl.program_id(0) + first) * inner + place, *views)
        return carry

    lax.fori_loop(0, inner, one, 0)


def entry_kernel(spacing, steps, step, features, centring, ones, gain, down, squeezed, *edges):
    centred = jnp.dot(strip(features), centring[...], preferred_element_type=F32)
    values = squeeze(centred, ones, gain[...], down[...]).reshape(squeezed.shape)
    squeezed[...] = values.astype(BF16)
    store_edges(values, edges, spacing, step, steps)


def middle_kernel(near, far, steps, step, centre, *rest):
    halos, rest = rest[:4], rest[4:]
    features, centring, ones, kernel, up, gain, down, stream_out, activated_out, squeezed, *rest = rest
    edges, (padded, taps) = rest[:4], rest[4:]
    columns = centre.shape[1]

    @pl.when(step == 0)
    def _():
        fill_padded(padded, centre, halos, near)

    activated = elu(convolve(padded, kernel, taps, near, step, columns)).astype(BF16)
    activated_out[...] = activated.reshape(activated_out.shape)
    stream = jnp.dot(strip(features), centring[...], preferred_element_type=F32) + widened(activated, up[...])
    stream_out[...] = stream.reshape(stream_out.shape)
    values = squeeze(stream, ones, gain[...], down[...]).reshape(squeezed.shape)
    squeezed[...] = values.astype(BF16)
    store_edges(values, edges, far, step, steps)


def head_kernel(near, steps, step, centre, *rest):
    halos, rest = rest[:4], rest[4:]
    stream_in, ones, kernel, up, gain, head, bias, stream_out, activated_out, by_row, *by_column, padded, taps = rest
    columns = centre.shape[1]

    @pl.when(step == 0)
    def _():
        fill_padded(padded, centre, halos, near)

    activated = elu(convolve(padded, kernel, taps, near, step, columns)).astype(BF16)
    activated_out[...] = activated.reshape(activated_out.shape)
    stream = strip(stream_in) + widened(activated, up[...])
    stream_out[...] = stream.reshape(stream_out.shape)
    standard, unused = standardize(stream, ones)
    entered = (standard * gain[...]).astype(BF16).reshape(2, ROWS, columns, stream.shape[1])
    pairs = jnp.concatenate([entered[0], entered[1]], axis=2).reshape(ROWS * columns, -1)
    logits = jnp.dot(pairs, head[...], preferred_element_type=F32) + bias[...]
    by_row[...] = logits.astype(BF16).reshape(by_row.shape)
    pairs = jnp.concatenate([entered[:, :, : columns // 2], entered[:, :, columns // 2 :]], axis=3)
    logits = jnp.dot(pairs.reshape(ROWS * columns, -1), head[...], preferred_element_type=F32) + bias[...]
    logits = logits.astype(BF16).reshape(2, ROWS, columns // 2, -1)
    place = 0
    for piece in by_column:
        piece[...] = logits[:, :, place : place + piece.shape[2]]
        place += piece.shape[2]


def loss_kernel(spacing, steps, inner, count, ends, step, by_row, *rest):
    facing, rest = rest[:count], rest[count:]
    targets, stream, activated, ones, head, group, up, *rest = rest
    *outputs, turned = rest
    grad_out, conv_out, left, right, *far = outputs[-4 - sum(ends) :]
    top = far[0] if ends[0] else None
    bottom = far[-1] if ends[1] else None
    edges = top, bottom, left, right

    @pl.when(step % inner == 0)
    def _():
        turned[...] = jnp.swapaxes(sum(array[...].astype(F32) for array in facing), 0, 1)

    start = (step % inner) * ROWS
    columns, lanes = by_row.shape[1:]
    symmetric = 0.5 * (by_row[...].astype(F32) + turned[pl.ds(start, ROWS)])
    exponent = jnp.exp(symmetric).reshape(ROWS * columns, lanes)
    upper = exponent.astype(BF16)
    lower = (exponent - upper.astype(F32)).astype(BF16)
    total = jnp.dot(upper, group[...], preferred_element_type=F32) + jnp.dot(
        lower, group[...], preferred_element_type=F32
    )
    logit_grad = (exponent / total - targets[...].astype(F32).reshape(exponent.shape)).astype(BF16)
    back = widened(logit_grad, head[...])
    standard, inverse = standardize(strip(stream), ones)
    grad = standardize_back(standard, inverse, back, ones)
    grad_out[...] = grad.reshape(grad_out.shape)
    values = jnp.dot(side_by_side(grad.astype(BF16)), up[...], preferred_element_type=F32)
    values = values * slope_from_elu(strip(activated).astype(F32))
    values = values.reshape(conv_out.shape)
    conv_out[...] = values.astype(BF16)
    store_edges(values, edges, spacing, step, steps)


def back_strip(spacing, step, centre, padded, taps, kernel, squeezed, down, centred, ones, gain, upstream):
    columns = centre.shape[1]
    lowered = convolve(padded, kernel, taps, spacing, step, columns)
    lowered = lowered * slope_from_elu(strip(squeezed).astype(F32))
    entered = stacked(jnp.dot(lowered.astype(BF16), down[...], preferred_element_type=F32))
    standard, inverse = standardize(centred, ones)
    scale = gain[...]
    entered = entered * (jnp.exp2(jnp.minimum(standard * (scale * math.log2(math.e)), 0.0)) * scale)
    entered = entered - jnp.sum(entered, -1, keepdims=True) * (1.0 / entered.shape[-1])
    return strip(upstream) + standardize_back(standard, inverse, entered, ones)


def back_kernel(near, far, steps, step, centre, *rest):
    halos, rest = rest[:4], rest[4:]
    kernel, squeezed, down, stream, ones, gain, upstream, activated, up, grad_out, conv_out, *rest = rest
    edges, (padded, taps) = rest[:4], rest[4:]

    @pl.when(step == 0)
    def _():
        fill_padded(padded, centre, halos, near)

    grad = back_strip(near, step, centre, padded, taps, kernel, squeezed, down, strip(stream), ones, gain, upstream)
    grad_out[...] = grad.reshape(grad_out.shape)
    values = jnp.dot(side_by_side(grad.astype(BF16)), up[...], preferred_element_type=F32)
    values = values * slope_from_elu(strip(activated).astype(F32))
    values = values.reshape(conv_out.shape)
    conv_out[...] = values.astype(BF16)
    store_edges(values, edges, far, step, steps)


def final_kernel(near, step, centre, *rest):
    halos, rest = rest[:4], rest[4:]
    kernel, squeezed, down, features, centring, ones, gain, upstream, grad_out, padded, taps = rest

    @pl.when(step == 0)
    def _():
        fill_padded(padded, centre, halos, near)

    centred = jnp.dot(strip(features), centring[...], preferred_element_type=F32)
    grad = back_strip(near, step, centre, padded, taps, kernel, squeezed, down, centred, ones, gain, upstream)
    grad_out[...] = grad.reshape(grad_out.shape)


def shifted(values, axis, move):
    count = lax.axis_size(axis)
    return lax.ppermute(values, axis, [(i, i + move) for i in range(count) if 0 <= i + move < count])


def exchange(edges):
    top, bottom, left, right = edges
    above = shifted(bottom, "row", 1)
    below = shifted(top, "row", -1)
    before = jnp.concatenate([right, above[:, -EDGE:], below[:, -EDGE:]], axis=0)
    after = jnp.concatenate([left, above[:, :EDGE], below[:, :EDGE]], axis=0)
    return above, below, shifted(before, "col", 1), shifted(after, "col", -1)


def facing_tile(tile):
    rows, cols = lax.axis_size("row"), lax.axis_size("col")
    if rows == cols:
        pairs = [(row * cols + col, col * cols + row) for row in range(rows) for col in range(cols)]
        return lax.ppermute(tile, ("row", "col"), pairs)
    if cols % rows:
        raise ValueError("unsupported mesh")
    times = cols // rows
    height = tile.shape[0] // times
    place = lax.axis_index("col") % times
    received = []
    for turn in range(times):
        piece = lax.dynamic_slice_in_dim(tile, ((place + turn) % times) * height, height, axis=0)
        pairs = [
            (row * cols + col, (col // times) * cols + times * row + (col % times + turn) % times)
            for row in range(rows)
            for col in range(cols)
        ]
        received.append(lax.ppermute(piece, ("row", "col"), pairs))
    stacked = jnp.stack(received)
    pieces = [
        lax.dynamic_index_in_dim(stacked, (place - source) % times, axis=0, keepdims=False)
        for source in range(times)
    ]
    return jnp.concatenate(pieces, axis=1)


def facing_logits(by_column):
    rows, cols = lax.axis_size("row"), lax.axis_size("col")
    if rows == cols and rows % 2 == 0:
        straight, *around = by_column
        places = [(row, col) for row in range(rows) for col in range(cols)]
        part = rows // 2
        far = [(row, col) for row, col in places if row // part != col // part]
        close = [(row, col) for row, col in places if row // part == col // part]
        number = lambda row, col: row * cols + col
        other = lambda row: (row + part) % rows
        move = lambda array, pairs: lax.ppermute(array, ("row", "col"), pairs)
        hops = [move(array, [(number(row, col), number(other(row), col)) for row, col in far]) for array in around]
        straight = move(straight, [(number(row, col), number(col, row)) for row, col in places])
        near = [move(array, [(number(row, col), number(col, row)) for row, col in close]) for array in around]
        hops = [move(array, [(number(other(row), col), number(col, row)) for row, col in far]) for array in hops]
        return [[straight]] + [list(pair) for pair in zip(hops, near)]
    tile = jnp.concatenate(by_column, axis=1)
    if rows == cols:
        tile = facing_tile(tile)
    else:
        bins = tile.shape[2] // 2
        tile = facing_tile(jnp.concatenate([tile[..., :bins], tile[..., bins:]], axis=1))
        half = tile.shape[1] // 2
        tile = jnp.concatenate([tile[:, :half], tile[:, half:]], axis=2)
    return [[tile]]


def diagonal(weight):
    zeros = jnp.zeros_like(weight)
    return jnp.concatenate(
        [jnp.concatenate([weight, zeros], axis=1), jnp.concatenate([zeros, weight], axis=1)], axis=0
    )


def dilated_weights(blocks):
    return jnp.concatenate(
        [jnp.concatenate([diagonal(block) for block in line], axis=1) for line in blocks], axis=0
    )


def two_parts(weight):
    centred = weight - jnp.mean(weight, axis=1, keepdims=True)
    upper = centred.astype(BF16).astype(F32)
    return jnp.concatenate([diagonal(upper), diagonal(centred - upper)], axis=0)


def derived(norm_gain, w_down, w_conv, w_up, w_head, head_bias):
    bins, channels = w_head.shape
    gains = [norm_gain[index : index + 1] * math.sqrt(channels) for index in range(3)]
    down_back = [w_down[index].astype(F32) for index in range(2)]
    up = [w_up[index].astype(F32) for index in range(2)]
    conv = [[[w_conv[index, row, col].astype(F32) for col in range(3)] for row in range(3)] for index in range(2)]
    back = [[[conv[index][2 - row][2 - col].T for col in range(3)] for row in range(3)] for index in range(2)]
    head_back = w_head[...].astype(F32)
    first = lax.broadcasted_iota(jnp.int32, (channels, channels), 0)
    second = lax.broadcasted_iota(jnp.int32, (channels, channels), 1)
    matrices = dict(
        downs=[diagonal(weight.T) for weight in down_back],
        downs_back=[diagonal(weight) for weight in down_back],
        ups=[two_parts(weight) for weight in up],
        ups_back=[diagonal(weight.T) for weight in up],
        convs=[dilated_weights(blocks) for blocks in conv],
        convs_back=[dilated_weights(blocks) for blocks in back],
        head=diagonal(head_back.T),
        head_back=two_parts(head_back * gains[2]),
        group=diagonal(jnp.ones((bins, bins), F32)),
        centring=jnp.where(first == second, 1.0, 0.0) - 1.0 / channels,
        ones=jnp.ones((channels, channels), F32),
    )
    matrices = jax.tree.map(lambda array: array.astype(BF16), matrices)
    bias = head_bias[...]
    return dict(matrices, gains=gains, bias=jnp.concatenate([bias, bias], axis=1))


def derive(*sources):
    shapes = jax.eval_shape(derived, *sources)
    leaves, tree = jax.tree.flatten(shapes)

    def kernel(*refs):
        results = jax.tree.leaves(derived(*refs[: len(sources)]))
        for ref, result in zip(refs[len(sources) :], results):
            ref[...] = result

    made = pl.pallas_call(
        kernel,
        grid=(1,),
        in_specs=[pl.BlockSpec(array.shape, lambda step, rank=array.ndim: (0,) * rank) for array in sources],
        out_specs=[pl.BlockSpec(leaf.shape, lambda step: (0, 0)) for leaf in leaves],
        out_shape=leaves,
        compiler_params=pltpu.CompilerParams(vmem_limit_bytes=60 * 1024 * 1024),
        name="weights",
    )(*sources)
    return jax.tree.unflatten(tree, made)


def shards(features, labels, norm_gain, w_down, w_conv, w_up, w_head, head_bias):
    rows, columns, channels = features.shape
    narrow = w_down.shape[2]
    bins = w_head.shape[1]
    half = rows // 2
    steps = half // ROWS
    lanes = 2 * narrow
    near, far = 4, 8

    made = derive(norm_gain, jnp.swapaxes(w_down, 1, 2), w_conv, w_up, w_head.T, head_bias[None])
    gains, bias, centring, ones, group = (made[name] for name in ("gains", "bias", "centring", "ones", "group"))
    downs, downs_back, ups, ups_back = (made[name] for name in ("downs", "downs_back", "ups", "ups_back"))
    convs, convs_back, head, head_back = (made[name] for name in ("convs", "convs_back", "head", "head_back"))

    def whole(array):
        zeros = (0,) * len(array.shape)
        return "whole", pl.BlockSpec(array.shape, lambda step: zeros)

    def strip_spec(width):
        return "halves", pl.BlockSpec((2, BLOCK, columns, width), lambda step: (0, step, 0, 0))

    def halves(dtype, width):
        return jax.ShapeDtypeStruct((2, half, columns, width), dtype)

    pair_spec = "rows", pl.BlockSpec((BLOCK, columns, lanes), lambda step: (step, 0, 0))
    pair_shape = jax.ShapeDtypeStruct((half, columns, lanes), BF16)

    def edges(spacing):
        shapes = [jax.ShapeDtypeStruct((spacing, columns // 2, lanes), BF16)] * 2
        shapes += [jax.ShapeDtypeStruct((half, EDGE, lanes), BF16)] * 2
        sides = "rows", pl.BlockSpec((BLOCK, EDGE, lanes), lambda step: (step, 0, 0))
        return shapes, [whole(shapes[0]), whole(shapes[1]), sides, sides]

    def scratch(spacing):
        width = columns + 2 * PAD
        return [
            pltpu.VMEM((half + 2 * spacing, width, lanes), BF16),
            pltpu.VMEM((ROWS, width, 3 * lanes), F32),
        ]

    def cost(convolutions, passes):
        pixels = rows * columns
        return pl.CostEstimate(
            flops=pixels * (convolutions * 18 * narrow * narrow + 4 * narrow * channels),
            bytes_accessed=pixels * channels * passes,
            transcendentals=pixels * channels,
        )

    def call(body, inputs, specs, shapes, out_specs, scratch_shapes, estimate, name):
        kinds = [kind for kind, spec in specs + out_specs] + ["whole"] * len(scratch_shapes)
        return pl.pallas_call(
            functools.partial(over_strips, body, kinds, 0),
            grid=(half // BLOCK,),
            in_specs=[spec for kind, spec in specs],
            out_specs=[spec for kind, spec in out_specs],
            out_shape=shapes,
            scratch_shapes=scratch_shapes,
            compiler_params=pltpu.CompilerParams(vmem_limit_bytes=56 * 1024 * 1024),
            cost_estimate=estimate,
            name=name,
        )(*inputs)

    own_labels = lax.all_to_all(labels, "col", split_axis=1, concat_axis=0, tiled=True)
    features, own_labels = lax.optimization_barrier((features, own_labels))
    split = features.reshape(2, half, columns, channels)
    bf_spec = strip_spec(channels)
    near_shapes, near_specs = edges(near)
    far_shapes, far_specs = edges(far)

    squeezed_1, *sent = call(
        functools.partial(entry_kernel, near, steps),
        (split, centring, ones, gains[0], downs[0]),
        [bf_spec] + [whole(array) for array in (centring, ones, gains[0], downs[0])],
        [pair_shape] + near_shapes,
        [pair_spec] + near_specs,
        [],
        cost(0, 4),
        "entry",
    )
    own_labels, *sent = lax.optimization_barrier((own_labels, *sent))
    facing_labels = facing_tile(own_labels)
    halos = exchange(sent)

    centre = squeezed_1
    stream_1, activated_1, squeezed_2, *sent = call(
        functools.partial(middle_kernel, near, far, steps),
        (centre, *halos, split, centring, ones, convs[0], ups[0], gains[1], downs[1]),
        [whole(centre)] + [whole(halo) for halo in halos] + [bf_spec]
        + [whole(array) for array in (centring, ones, convs[0], ups[0], gains[1], downs[1])],
        [halves(F32, channels), pair_shape, pair_shape] + far_shapes,
        [strip_spec(channels), pair_spec, pair_spec] + far_specs,
        scratch(near),
        cost(1, 12),
        "middle",
    )
    facing_labels, *sent = lax.optimization_barrier((facing_labels, *sent))
    facing_labels = facing_labels.T
    halos = exchange(sent)

    centre = squeezed_2
    by_row_spec = "rows", pl.BlockSpec((BLOCK, columns, 2 * bins), lambda step: (step, 0, 0))
    parts = [columns // 4, columns // 8, columns // 8]
    stream_2, activated_2, by_row, *by_column = call(
        functools.partial(head_kernel, far, steps),
        (centre, *halos, stream_1, ones, convs[1], ups[1], gains[2], head, bias),
        [whole(centre)] + [whole(halo) for halo in halos] + [bf_spec]
        + [whole(array) for array in (ones, convs[1], ups[1], gains[2], head, bias)],
        [
            halves(F32, channels),
            pair_shape,
            jax.ShapeDtypeStruct((half, columns, 2 * bins), BF16),
            *(jax.ShapeDtypeStruct((2, half, part, 2 * bins), BF16) for part in parts),
        ],
        [
            strip_spec(channels),
            pair_spec,
            by_row_spec,
            *(("halves", pl.BlockSpec((2, BLOCK, part, 2 * bins), lambda step: (0, step, 0, 0))) for part in parts),
        ],
        scratch(far),
        cost(1, 14),
        "head",
    )
    facing = facing_logits([piece.reshape(rows, piece.shape[2], 2 * bins) for piece in by_column])

    numbers = jnp.arange(bins, dtype=jnp.int32)

    def onehot(values):
        return (values[:, :, None] == numbers).astype(F32)

    targets = jnp.concatenate(
        [
            0.5 * (onehot(own_labels[part]) + onehot(facing_labels[part]))
            for part in (slice(0, half), slice(half, rows))
        ],
        axis=2,
    ).astype(BF16)

    taken = 0
    outputs = []
    sent = [None, None, None, None]
    for index, piece in enumerate(facing):
        blocks = piece[0].shape[1] // BLOCK
        ends = taken == 0, index == len(facing) - 1

        def moved(spec, first=taken):
            kind, block = spec
            return kind, pl.BlockSpec(
                block.block_shape,
                lambda step: tuple(
                    place + first * (rank == (1 if kind == "halves" else 0))
                    for rank, place in enumerate(block.index_map(step))
                ),
            )

        weights = [ones, head_back, group, ups_back[1]]
        side_shape, side_spec = far_shapes[2], moved(far_specs[2])
        specs = [moved(by_row_spec)]
        specs += [("whole", pl.BlockSpec((columns, BLOCK, 2 * bins), lambda step: (0, step, 0)))] * len(piece)
        specs += [moved(by_row_spec), moved(bf_spec), moved(pair_spec)] + [whole(array) for array in weights]
        inputs = [by_row, *piece, targets, stream_2, activated_2, *weights]
        out_shapes = [halves(F32, channels), pair_shape, side_shape, side_shape]
        out_specs = [moved(bf_spec), moved(pair_spec), side_spec, side_spec]
        for place in range(2):
            if ends[place]:
                out_shapes.append(far_shapes[place])
                out_specs.append(far_specs[place])
        kinds = [kind for kind, spec in specs] + ["whole"] * len(outputs)
        kinds += [kind for kind, spec in out_specs] + ["whole"]
        body = functools.partial(loss_kernel, far, steps, BLOCK // ROWS, len(piece), ends)
        results = pl.pallas_call(
            functools.partial(over_strips, body, kinds, taken),
            grid=(blocks,),
            in_specs=[spec for kind, spec in specs] + [pl.BlockSpec(memory_space=pl.ANY)] * len(outputs),
            out_specs=[spec for kind, spec in out_specs],
            out_shape=out_shapes,
            input_output_aliases={len(inputs) + place: place for place in range(len(outputs))},
            scratch_shapes=[pltpu.VMEM((BLOCK, columns, 2 * bins), F32)],
            compiler_params=pltpu.CompilerParams(vmem_limit_bytes=56 * 1024 * 1024),
            cost_estimate=cost(0, 18),
            name="loss",
        )(*inputs, *outputs)
        outputs = list(results[:4])
        if ends[0]:
            sent[0] = results[4]
        if ends[1]:
            sent[1] = results[-1]
        taken += blocks
    grad_2, conv_grad_2, *sent[2:] = outputs
    halos = exchange(sent)

    centre = conv_grad_2
    grad_1, conv_grad_1, *sent = call(
        functools.partial(back_kernel, far, near, steps),
        (centre, *halos, convs_back[1], squeezed_2, downs_back[1], stream_1, ones, gains[1], grad_2, activated_1, ups_back[0]),
        [whole(centre)] + [whole(halo) for halo in halos]
        + [
            whole(convs_back[1]),
            pair_spec,
            whole(downs_back[1]),
            bf_spec,
            whole(ones),
            whole(gains[1]),
            bf_spec,
            pair_spec,
            whole(ups_back[0]),
        ],
        [halves(F32, channels), pair_shape] + near_shapes,
        [strip_spec(channels), pair_spec] + near_specs,
        scratch(far),
        cost(1, 20),
        "back",
    )
    halos = exchange(sent)

    centre = conv_grad_1
    (grad_0,) = call(
        functools.partial(final_kernel, near),
        (centre, *halos, convs_back[0], squeezed_1, downs_back[0], split, centring, ones, gains[0], grad_1),
        [whole(centre)] + [whole(halo) for halo in halos]
        + [
            whole(convs_back[0]),
            pair_spec,
            whole(downs_back[0]),
            bf_spec,
            whole(centring),
            whole(ones),
            whole(gains[0]),
            bf_spec,
        ],
        [halves(F32, channels)],
        [strip_spec(channels)],
        scratch(near),
        cost(1, 16),
        "final",
    )
    return grad_0.reshape(features.shape)


def solution(mesh):
    return jax.shard_map(
        shards,
        mesh=mesh,
        in_specs=(
            P(("dp", "row"), "col", None),
            P(("dp", "row", "col"), None),
            P(),
            P(),
            P(),
            P(),
            P(),
            P(),
        ),
        out_specs=P(("dp", "row"), "col", None),
        check_vma=False,
    )
```
